32 devices in a mesh: shot: 2 (over core), gx: 4 (over y, x), gy: 4 (over z).
Axes of the slice: x: 2, y: 2, z: 4, core: 2. Of those that a mesh axis runs over, the one named last changes fastest.
Arguments:
- stress_fields: float32 [4, 3, 6, 64, 64, 128], P('shot', None, None, 'gx', 'gy'), may hold values from -6 to 6
- velocity_fields: float32 [4, 3, 3, 64, 64, 128], P('shot', None, None, 'gx', 'gy'), may hold values from -6 to 6
- lame: float32 [64, 64, 128], P('gx', 'gy'), may hold values from 0.4 to 1.6
- shear: float32 [64, 64, 128], P('gx', 'gy'), may hold values from 0.25 to 1
- density: float32 [64, 64, 128], P('gx', 'gy'), may hold values from 0.8 to 2
- lame_change: float32 [64, 64, 128], P('gx', 'gy'), may hold values from -3 to 3
- shear_change: float32 [64, 64, 128], P('gx', 'gy'), may hold values from -3 to 3
- density_change: float32 [64, 64, 128], P('gx', 'gy'), may hold values from -3 to 3
- source_cell: int32 [4], P('shot'), may hold values from 0 to 524287
- source_amp: float32 [4], P('shot'), may hold values from 4 to 16
- receiver_cell: int32 [4, 512], P('shot'), may hold values from 0 to 4095
Outputs:
- new_velocity: float32 [4, 2, 3, 64, 64, 128], P('shot', None, None, 'gx', 'gy')
- new_stress: float32 [4, 2, 6, 64, 64, 128], P('shot', None, None, 'gx', 'gy')
- kernels: float32 [3, 64, 64, 128], P(None, ('gx', 'shot'), 'gy')
The draws below stay inside these ranges and needn't reach their ends.
Inputs may be any that keep to these rules, and one draw needn't show every extreme that they name: source_cell[s] = x * 64 * 128 + y * 128 + z for the source's grid cell (x, y, z). receiver_cell[s, r] = x * 64 + y for a receiver at (x, y, 2); several receivers of a shot may share a cell.
All inputs are finite; a program needn't handle non-finite values.
Results may differ from the reference program's by a relative error of at most 0.0003.
Values sent between devices are 32-bit elements; how exact they have to be, the bound alone decides.
A program may use at most 128 MiB of HBM per device.

```python
import math
import jax
import jax.numpy as jnp
from jax import lax

NZ = 128
REC = 512
RDEPTH = 2
NX = 64
NY = 64
SHOTS = 4


def place_ends(values, own_key, low, high):
    longest = values.shape.index(max(values.shape))
    spots = []
    for shift in (0, 1):
        where = [jax.random.randint(jax.random.fold_in(own_key, axis), (), 0, length) for axis, length in enumerate(values.shape)]
        where[longest] = (where[longest] + shift) % values.shape[longest]
        spots.append(tuple(where))
    return values.at[spots[0]].set(low).at[spots[1]].set(high)


def level_of(rng, shape, split, smallest, high):
    level, own = 1.0, jax.random.fold_in(rng, 6)
    for position, blocks in split:
        heights = jnp.exp(jax.random.uniform(jax.random.fold_in(own, position), (blocks,), jnp.float32, smallest / len(split), high / len(split)))
        level = level * jnp.repeat(heights, shape[position] // blocks).reshape([-1 if axis == position else 1 for axis in range(len(shape))])
    return level


def normal_values(key, extent, spread, most, split=(), kind=jnp.bfloat16):
    level = level_of(key, extent, split, -0.22, 0.18) if split else 1.0
    values = jax.random.normal(key, extent, jnp.float32) * spread * level
    return jnp.minimum(jnp.maximum(values, -most), most).astype(kind)


def setup_inputs(seed: int = 0) -> dict:
    streams_of = jax.random.split(jax.random.key(seed), 12)
    return {
        "stress_fields": normal_values(streams_of[0], (SHOTS, 3, 6, NX, NY, NZ), 1.0, 6.0, ((0, 2), (3, 4), (4, 4)), jnp.float32),
        "velocity_fields": normal_values(streams_of[1], (SHOTS, 3, 3, NX, NY, NZ), 1.0, 6.0, ((0, 2), (3, 4), (4, 4)), jnp.float32),
        "lame": jnp.clip(jnp.exp(math.log(1.6) - 1.3862944 * jax.random.uniform(streams_of[2], (NX, NY, NZ), jnp.float32) ** level_of(streams_of[2], (NX, NY, NZ), ((0, 4), (1, 4)), -0.2, 0.2)), 0.4, 1.6),
        "shear": jnp.clip(jnp.exp(math.log(1.0) - 1.3862944 * jax.random.uniform(streams_of[3], (NX, NY, NZ), jnp.float32) ** level_of(streams_of[3], (NX, NY, NZ), ((0, 4), (1, 4)), -0.2, 0.2)), 0.25, 1.0),
        "density": jnp.clip(jnp.exp(math.log(2.0) - 0.9162907 * jax.random.uniform(streams_of[4], (NX, NY, NZ), jnp.float32) ** level_of(streams_of[4], (NX, NY, NZ), ((0, 4), (1, 4)), -0.2, 0.2)), 0.8, 2.0),
        "lame_change": normal_values(streams_of[5], (NX, NY, NZ), 0.5, 3.0, ((0, 4), (1, 4)), jnp.float32),
        "shear_change": normal_values(streams_of[6], (NX, NY, NZ), 0.5, 3.0, ((0, 4), (1, 4)), jnp.float32),
        "density_change": normal_values(streams_of[7], (NX, NY, NZ), 0.5, 3.0, ((0, 4), (1, 4)), jnp.float32),
        "source_cell": place_ends(jax.random.randint(streams_of[8], (SHOTS,), 0, NX * NY * NZ), jax.random.fold_in(streams_of[8], 1), 0, (NX * NY * NZ) - 1).astype(jnp.int32),
        "source_amp": jnp.clip(jnp.exp(math.log(16.0) - 1.3862944 * jax.random.uniform(streams_of[9], (SHOTS,), jnp.float32) ** level_of(streams_of[9], (SHOTS,), ((0, 2),), -0.2, 0.2)), 4.0, 16.0),
        "receiver_cell": place_ends(jax.random.randint(streams_of[10], (SHOTS, REC), 0, NX * NY), jax.random.fold_in(streams_of[10], 1), 0, (NX * NY) - 1).astype(jnp.int32),
    }


courant = 0.25
stress_upper_rows = (0,)
stress_lower_rows = (3, 4)
stress_upper_columns = (1,)
stress_lower_columns = (3, 5)
motion_upper_rows = (1, 2)
motion_lower_rows = (0,)
motion_upper_columns = (0, 2)
motion_lower_columns = (1,)


def forward_rows(quantity, upper_face):
    return jnp.concatenate([quantity[..., 1:, :, :], upper_face], axis=-3) - quantity


def backward_rows(quantity, lower_face):
    return quantity - jnp.concatenate([lower_face, quantity[..., :-1, :, :]], axis=-3)


def forward_columns(quantity, upper_face):
    return jnp.concatenate([quantity[..., 1:, :], upper_face], axis=-2) - quantity


def backward_columns(quantity, lower_face):
    return quantity - jnp.concatenate([lower_face, quantity[..., :-1, :]], axis=-2)


def forward_depth(quantity):
    return jnp.concatenate([quantity[..., 1:], jnp.zeros_like(quantity[..., :1])], axis=-1) - quantity


def backward_depth(quantity):
    return quantity - jnp.concatenate([jnp.zeros_like(quantity[..., :1]), quantity[..., :-1]], axis=-1)


def component(array, index):
    return array[..., index, :, :, :]


def wavefield(array, index):
    return array[..., index, :, :, :, :]


def accelerations(stress, upper_rows, lower_rows, upper_columns, lower_columns):
    accel_x = forward_rows(component(stress, 0), component(upper_rows, 0)) + backward_columns(component(stress, 3), component(lower_columns, 0)) + backward_depth(component(stress, 4))
    accel_y = backward_rows(component(stress, 3), component(lower_rows, 0)) + forward_columns(component(stress, 1), component(upper_columns, 0)) + backward_depth(component(stress, 5))
    accel_z = backward_rows(component(stress, 4), component(lower_rows, 1)) + backward_columns(component(stress, 5), component(lower_columns, 1)) + forward_depth(component(stress, 2))
    return jnp.stack([accel_x, accel_y, accel_z], axis=-4)


def strains(velocity, upper_rows, lower_rows, upper_columns, lower_columns):
    strain_xx = backward_rows(component(velocity, 0), component(lower_rows, 0))
    strain_yy = backward_columns(component(velocity, 1), component(lower_columns, 0))
    strain_zz = backward_depth(component(velocity, 2))
    shear_xy = forward_columns(component(velocity, 0), component(upper_columns, 0)) + forward_rows(component(velocity, 1), component(upper_rows, 0))
    shear_xz = forward_depth(component(velocity, 0)) + forward_rows(component(velocity, 2), component(upper_rows, 1))
    shear_yz = forward_depth(component(velocity, 1)) + forward_columns(component(velocity, 2), component(upper_columns, 1))
    return jnp.stack([strain_xx, strain_yy, strain_zz, shear_xy, shear_xz, shear_yz], axis=-4)


def moduli(strain, first, second):
    trace = component(strain, 0) + component(strain, 1) + component(strain, 2)
    parts = [first * trace + 2.0 * second * component(strain, index) for index in range(3)]
    parts = parts + [second * component(strain, index) for index in range(3, 6)]
    return jnp.stack(parts, axis=-4)


def update_velocity(velocity, accel, buoyancy, density_change, source_field, record_field):
    scaled = courant * buoyancy
    base = wavefield(velocity, 0) + scaled * wavefield(accel, 0)
    base = base.at[..., 2, :, :, :].add(scaled * source_field)
    born = wavefield(velocity, 1) + scaled * (wavefield(accel, 1) - density_change * buoyancy * wavefield(accel, 0))
    adjoint = wavefield(velocity, 2) + scaled * wavefield(accel, 2)
    adjoint = adjoint.at[..., 2, :, :, :].add(scaled * record_field * component(born, 2))
    return jnp.stack([base, born, adjoint], axis=-5)


def update_stress(stress, strain, lame, shear, lame_change, shear_change):
    born = wavefield(stress, 1) + courant * (moduli(wavefield(strain, 1), lame, shear) + moduli(wavefield(strain, 0), lame_change, shear_change))
    adjoint = wavefield(stress, 2) + courant * moduli(wavefield(strain, 2), lame, shear)
    return jnp.stack([born, adjoint], axis=-5)


def kernel_terms(strain, new_stress, accel, velocity_next, buoyancy):
    base_strain = wavefield(strain, 0)
    adjoint_stress = wavefield(new_stress, 1)
    trace_product = (component(base_strain, 0) + component(base_strain, 1) + component(base_strain, 2)) * (component(adjoint_stress, 0) + component(adjoint_stress, 1) + component(adjoint_stress, 2))
    shear_sum = 2.0 * (component(base_strain, 0) * component(adjoint_stress, 0) + component(base_strain, 1) * component(adjoint_stress, 1) + component(base_strain, 2) * component(adjoint_stress, 2))
    shear_sum = shear_sum + component(base_strain, 3) * component(adjoint_stress, 3) + component(base_strain, 4) * component(adjoint_stress, 4) + component(base_strain, 5) * component(adjoint_stress, 5)
    density_sum = buoyancy * jnp.sum(wavefield(accel, 0) * wavefield(velocity_next, 2), axis=-4)
    return jnp.stack([trace_product, shear_sum, density_sum], axis=-4)


def zero_faces(fields, upper_rows, lower_rows, upper_columns, lower_columns):
    leading = fields.shape[:-4]
    rows, cols, depth = fields.shape[-3:]
    return (jnp.zeros(leading + (len(upper_rows), 1, cols, depth), fields.dtype),
            jnp.zeros(leading + (len(lower_rows), 1, cols, depth), fields.dtype),
            jnp.zeros(leading + (len(upper_columns), rows, 1, depth), fields.dtype),
            jnp.zeros(leading + (len(lower_columns), rows, 1, depth), fields.dtype))


def reference(stress_fields, velocity_fields, lame, shear, density, lame_change, shear_change, density_change, source_cell, source_amp, receiver_cell):
    rows, cols, depth = lame.shape
    real_type = lame.dtype
    buoyancy = 1.0 / density
    row_ids = jnp.arange(rows, dtype=jnp.int32)
    column_ids = jnp.arange(cols, dtype=jnp.int32)
    depth_ids = jnp.arange(depth, dtype=jnp.int32)
    plane = (depth_ids == RDEPTH).astype(real_type)

    def one_shot(total, inputs):
        stress, velocity, cell, amplitude, receivers = inputs
        source_row = cell // (cols * depth)
        source_column = (cell // depth) % cols
        source_level = cell % depth
        source_field = amplitude * (row_ids == source_row).astype(real_type)[:, None, None] * (column_ids == source_column).astype(real_type)[None, :, None] * (depth_ids == source_level).astype(real_type)[None, None, :]
        receiver_rows = receivers // cols
        receiver_columns = receivers % cols
        row_marks = (receiver_rows[:, None] == row_ids[None, :]).astype(real_type)
        column_marks = (receiver_columns[:, None] == column_ids[None, :]).astype(real_type)
        counts = jnp.dot(row_marks.T, column_marks, precision=lax.Precision.HIGHEST, preferred_element_type=jnp.float32)
        record_field = counts[:, :, None] * plane
        accel = accelerations(stress, *zero_faces(stress, stress_upper_rows, stress_lower_rows, stress_upper_columns, stress_lower_columns))
        velocity_next = update_velocity(velocity, accel, buoyancy, density_change, source_field, record_field)
        strain = strains(velocity_next, *zero_faces(velocity_next, motion_upper_rows, motion_lower_rows, motion_upper_columns, motion_lower_columns))
        new_stress = update_stress(stress, strain, lame, shear, lame_change, shear_change)
        terms = kernel_terms(strain, new_stress, accel, velocity_next, buoyancy)
        return total + terms, (velocity_next[1:], new_stress)

    start = jnp.zeros((3, rows, cols, depth), jnp.float32)
    total, outputs = lax.scan(one_shot, start, (stress_fields, velocity_fields, source_cell, source_amp, receiver_cell))
    return outputs[0], outputs[1], total / SHOTS
```

```python
import functools

import jax
import jax.numpy as jnp
from jax import lax
from jax.experimental import pallas as pl
from jax.experimental.pallas import tpu as pltpu
from jax.sharding import PartitionSpec as P

RDEPTH = 2
COURANT = 0.25
MESH = pl.DeviceIdType.MESH
VMEM_LIMIT = 32 * 1024 * 1024


def shifted_up(tile, halo, axis):
    length = tile.shape[axis]
    index = lax.broadcasted_iota(jnp.int32, tile.shape, axis)
    return jnp.where(index == length - 1, halo, pltpu.roll(tile, length - 1, axis))


def shifted_down(tile, halo, axis):
    index = lax.broadcasted_iota(jnp.int32, tile.shape, axis)
    return jnp.where(index == 0, halo, pltpu.roll(tile, 1, axis))


def step_kernel(
    every_column,
    total_shots,
    stress,
    velocity,
    lame_in,
    shear_in,
    density_in,
    lame_change_in,
    shear_change_in,
    density_change_in,
    receivers_in,
    source_cell,
    source_amp,
    st,
    mo,
    kernels,
    params,
    receivers,
    record,
    record_row,
    record_col,
    accel0,
    terms,
    first_stress,
    last_stress,
    left_stress,
    right_stress,
    first_motion,
    last_motion,
    left_motion,
    right_motion,
    low_out,
    up_out,
    left_out,
    right_out,
    from_up,
    from_low,
    from_right,
    from_left,
    corner_out,
    corner_in,
    edge_out,
    edge_in,
    low_halo,
    up_halo,
    left_halo,
    right_halo,
    landed,
    load_sem,
    face_sem,
    param_sem,
    send_sem,
    recv_sem,
    share_send_sem,
    share_recv_sem,
):
    shots, waves, _, rows, cols, depth = stress.shape
    gx, gy = lax.axis_index("gx"), lax.axis_index("gy")
    nx, ny = lax.axis_size("gx"), lax.axis_size("gy")
    me, groups = lax.axis_index("shot"), lax.axis_size("shot")
    own = rows // groups
    has_low_x, has_up_x = gx > 0, gx < nx - 1
    has_low_y, has_up_y = gy > 0, gy < ny - 1
    sides = (
        (has_low_x, {"gx": gx - 1}),
        (has_up_x, {"gx": gx + 1}),
        (has_low_y, {"gy": gy - 1}),
        (has_up_y, {"gy": gy + 1}),
    )
    barrier = pltpu.get_barrier_semaphore()
    for present, device in sides:

        @pl.when(present)
        def _(device=device):
            pl.semaphore_signal(barrier, inc=1, device_id=device, device_id_type=MESH)

    for k in range(1, groups):
        peer = lax.rem(me + k, groups)
        pl.semaphore_signal(barrier, inc=1, device_id={"shot": peer}, device_id_type=MESH)

    tail = 2 + shots * 7
    faces = (
        (stress.at[:, :, :, 0], first_stress),
        (stress.at[:, :, :, rows - 1], last_stress),
        (velocity.at[:, :, pl.ds(1, 2), 0], first_motion),
        (velocity.at[:, :, 0, rows - 1], last_motion),
        (density_in.at[0], low_out.at[0]),
        (density_change_in.at[0], low_out.at[1]),
        (density_in.at[rows - 1], up_out.at[0]),
        (density_change_in.at[rows - 1], up_out.at[1]),
        (stress.at[:, :, :, :, 0], left_stress),
        (stress.at[:, :, :, :, cols - 1], right_stress),
        (velocity.at[:, :, 0, :, 0], left_motion.at[0]),
        (velocity.at[:, :, 2, :, 0], left_motion.at[1]),
        (velocity.at[:, :, 1, :, cols - 1], right_motion),
        (density_in.at[:, 0], left_out.at[0]),
        (density_change_in.at[:, 0], left_out.at[1]),
        (density_in.at[:, cols - 1], right_out.at[0]),
        (density_change_in.at[:, cols - 1], right_out.at[1]),
    )
    face_loads = [
        pltpu.make_async_copy(src, dst, face_sem.at[i]) for i, (src, dst) in enumerate(faces)
    ]
    stress_loads = [
        pltpu.make_async_copy(stress.at[s], st.at[s], load_sem.at[s, 0]) for s in range(shots)
    ]
    motion_loads = [
        pltpu.make_async_copy(velocity.at[s], mo.at[s], load_sem.at[s, 1]) for s in range(shots)
    ]
    receiver_load = pltpu.make_async_copy(receivers_in, receivers, param_sem.at[6])
    sources = (density_in, density_change_in, lame_in, shear_in, lame_change_in, shear_change_in)
    param_loads = [
        pltpu.make_async_copy(source, params.at[i], param_sem.at[i])
        for i, source in enumerate(sources)
    ]
    for copy in face_loads:
        copy.start()
    receiver_load.start()
    density, density_change, lame, shear, lame_change, shear_change = (
        params.at[i] for i in range(6)
    )

    def face(src, dst, slot, device):
        return pltpu.make_async_remote_copy(
            src_ref=src,
            dst_ref=dst,
            send_sem=send_sem.at[slot],
            recv_sem=recv_sem.at[slot],
            device_id=device,
            device_id_type=MESH,
        )

    low_x, up_x, low_y, up_y = (device for _, device in sides)
    body, rest = pl.ds(0, tail), pl.ds(tail, shots * 2)
    row_faces = (
        (face(low_out.at[body], from_up.at[body], 0, low_x), has_low_x, has_up_x),
        (face(up_out.at[body], from_low.at[body], 1, up_x), has_up_x, has_low_x),
    )
    born_faces = (
        (face(low_out.at[rest], from_up.at[rest], 8, low_x), has_low_x, has_up_x),
        (face(up_out.at[rest], from_low.at[rest], 9, up_x), has_up_x, has_low_x),
    )
    col_faces = (
        (face(left_out, from_right, 2, low_y), has_low_y, has_up_y),
        (face(right_out, from_left, 3, up_y), has_up_y, has_low_y),
    )
    corners = (
        (face(corner_out.at[0], corner_in.at[0], 4, low_x), has_low_x, has_up_x),
        (face(corner_out.at[1], corner_in.at[1], 5, up_x), has_up_x, has_low_x),
    )
    edges = (
        (face(edge_out.at[0], edge_in.at[0], 6, low_y), has_low_y, has_up_y),
        (face(edge_out.at[1], edge_in.at[1], 7, up_y), has_up_y, has_low_y),
    )

    def send(faces):
        for copy, sends, _ in faces:

            @pl.when(sends)
            def _(copy=copy):
                copy.start()

    def sent(faces):
        for copy, sends, _ in faces:

            @pl.when(sends)
            def _(copy=copy):
                copy.wait_send()

    def received(faces):
        for copy, _, comes in faces:

            @pl.when(comes)
            def _(copy=copy):
                copy.wait_recv()

    row_start, col_start = gx * rows, gy * cols
    pairs = [(s, w) for s in range(shots) for w in range(waves)]
    every = slice(None)

    def slot(s, w, i):
        return (s * waves + w) * 3 + i

    def spot(s, w, i, early):
        if w != 1:
            return 2 + s * 7 + (w // 2) * 3 + i
        if i == early:
            return 2 + s * 7 + 6
        return tail + s * 2 + i // (3 - early)

    def to_low(s, w, i):
        return spot(s, w, i, 2)

    def to_up(s, w, i):
        return spot(s, w, i, 1)

    def scales(message):
        buoyancy = 1.0 / message[0]
        return COURANT * buoyancy, message[1] * buoyancy

    def source_of(s, here):
        return jnp.where(here == source_cell[s], source_amp[s], 0.0)

    def advance(scaled, change, w, start, push):
        if w == 1:
            return start + scaled * (push[1] - change * push[0])
        return start + scaled * push[w]

    place = (
        lax.broadcasted_iota(jnp.int32, (cols, depth), 0) + col_start
    ) * depth + lax.broadcasted_iota(jnp.int32, (cols, depth), 1)
    side_place = (
        (lax.broadcasted_iota(jnp.int32, (rows, depth), 0) + row_start) * every_column + col_start
    ) * depth + lax.broadcasted_iota(jnp.int32, (rows, depth), 1)

    for copy in face_loads[:8]:
        copy.wait()
    low_scales, up_scales = scales(low_out), scales(up_out)
    for s in range(shots):
        push_y, push_z, push_x = [], [], []
        for w in range(waves):
            sxx, syy, szz, sxy, sxz, syz = (first_stress[s, w, i] for i in range(6))
            low_out[to_low(s, w, 0)] = sxx
            push_y.append(sxy + (shifted_up(syy, 0.0, 0) - syy) + (syz - shifted_down(syz, 0.0, 1)))
            push_z.append(sxz + (syz - shifted_down(syz, 0.0, 0)) + (shifted_up(szz, 0.0, 1) - szz))
            sxx, sxy, sxz = (last_stress[s, w, i] for i in (0, 3, 4))
            up_out[to_up(s, w, 0)] = sxy
            up_out[to_up(s, w, 1)] = sxz
            push_x.append((sxy - shifted_down(sxy, 0.0, 0)) + (sxz - shifted_down(sxz, 0.0, 1)) - sxx)
        here = place + row_start * (every_column * depth)
        for w in range(waves):
            low_out[to_low(s, w, 1)] = advance(*low_scales, w, first_motion[s, w, 0], push_y)
            moved = advance(*low_scales, w, first_motion[s, w, 1], push_z)
            if w == 0:
                moved = moved + low_scales[0] * source_of(s, here)
            low_out[to_low(s, w, 2)] = moved
            up_out[to_up(s, w, 2)] = advance(*up_scales, w, last_motion[s, w], push_x)

    for copy in face_loads[8:]:
        copy.wait()
    left_scales, right_scales = scales(left_out), scales(right_out)
    for s in range(shots):
        push_x, push_z, push_y = [], [], []
        for w in range(waves):
            sxx, syy, szz, sxy, sxz, syz = (left_stress[s, w, i] for i in range(6))
            left_out[to_low(s, w, 0)] = syy
            push_x.append((shifted_up(sxx, 0.0, 0) - sxx) + sxy + (sxz - shifted_down(sxz, 0.0, 1)))
            push_z.append((sxz - shifted_down(sxz, 0.0, 0)) + syz + (shifted_up(szz, 0.0, 1) - szz))
            syy, sxy, syz = (right_stress[s, w, i] for i in (1, 3, 5))
            right_out[to_up(s, w, 0)] = sxy
            right_out[to_up(s, w, 1)] = syz
            push_y.append((sxy - shifted_down(sxy, 0.0, 0)) + (syz - shifted_down(syz, 0.0, 1)) - syy)
        for w in range(waves):
            left_out[to_low(s, w, 1)] = advance(*left_scales, w, left_motion[0, s, w], push_x)
            moved = advance(*left_scales, w, left_motion[1, s, w], push_z)
            if w == 0:
                moved = moved + left_scales[0] * source_of(s, side_place)
            left_out[to_low(s, w, 2)] = moved
            right_out[to_up(s, w, 2)] = advance(*right_scales, w, right_motion[s, w], push_y)

    def line(n):
        return pl.ds(n, 1)

    first, last = line(0), line(cols - 1)
    for s, w in pairs:
        corner_out[0, line(slot(s, w, 0)), :] = first_stress[s, w, 1, first, :]
        corner_out[0, line(slot(s, w, 1)), :] = first_stress[s, w, 0, first, :]
        corner_out[0, line(slot(s, w, 2)), :] = first_stress[s, w, 5, last, :]
        corner_out[1, line(slot(s, w, 0)), :] = last_stress[s, w, 3, last, :]
        corner_out[1, line(slot(s, w, 1)), :] = last_stress[s, w, 4, first, :]

    neighbours = groups - 1
    for present, _ in sides:
        neighbours = neighbours + present.astype(jnp.int32)
    pl.semaphore_wait(barrier, neighbours)
    send(corners)
    send(row_faces)
    send(col_faces)
    send(born_faces)
    param_loads[0].start()
    param_loads[1].start()
    for s in range(shots):
        stress_loads[s].start()
        motion_loads[s].start()
    for copy in param_loads[2:]:
        copy.start()

    for comes, ref in (
        (has_up_x, corner_in.at[0]),
        (has_low_x, corner_in.at[1]),
        (has_up_y, edge_in.at[0]),
        (has_low_y, edge_in.at[1]),
        (has_up_x, up_halo),
        (has_low_x, low_halo),
        (has_up_y, right_halo),
        (has_low_y, left_halo),
    ):

        @pl.when(jnp.logical_not(comes))
        def _(ref=ref):
            ref[...] = jnp.zeros(ref.shape, jnp.float32)

    receiver_load.wait()
    count = receivers.shape[1]
    plane = (lax.broadcasted_iota(jnp.int32, (count, depth), 1) == RDEPTH).astype(jnp.bfloat16)

    def count_at(s, cell):
        marks = jnp.where(receivers[pl.ds(s, 1), :] == cell, 1.0, 0.0).astype(jnp.bfloat16)
        return jnp.dot(marks, plane, preferred_element_type=jnp.float32)

    cell = (
        lax.broadcasted_iota(jnp.int32, (rows, cols, count), 0) + row_start
    ) * every_column + (lax.broadcasted_iota(jnp.int32, (rows, cols, count), 1) + col_start)
    cell = cell.reshape(rows * cols, count)
    next_row = (row_start + rows) * every_column + (
        lax.broadcasted_iota(jnp.int32, (cols, count), 0) + col_start
    )
    next_col = (lax.broadcasted_iota(jnp.int32, (rows, count), 0) + row_start) * every_column + (
        col_start + cols
    )
    for s in range(shots):
        record[s] = count_at(s, cell).reshape(rows, cols, depth)
        record_row[s] = count_at(s, next_row)
        record_col[s] = count_at(s, next_col)

    def motion(s):
        target, amplitude = source_cell[s], source_amp[s]

        def motion_row(x, carry):
            after = lax.rem(x + 1, rows)
            before = lax.rem(x + rows - 1, rows)
            last, first = x == rows - 1, x == 0
            buoyancy = 1.0 / density[x]
            scaled = COURANT * buoyancy
            change = density_change[x] * buoyancy
            accel = []
            for w in range(waves):
                sxx, syy, szz = st[s, w, 0, x], st[s, w, 1, x], st[s, w, 2, x]
                sxy, sxz, syz = st[s, w, 3, x], st[s, w, 4, x], st[s, w, 5, x]
                sxx_after = jnp.where(last, 0.0, st[s, w, 0, after])
                sxy_before = jnp.where(first, 0.0, st[s, w, 3, before])
                sxz_before = jnp.where(first, 0.0, st[s, w, 4, before])
                accel.append(
                    (
                        (sxx_after - sxx)
                        + (sxy - shifted_down(sxy, 0.0, 0))
                        + (sxz - shifted_down(sxz, 0.0, 1)),
                        (sxy - sxy_before)
                        + (shifted_up(syy, 0.0, 0) - syy)
                        + (syz - shifted_down(syz, 0.0, 1)),
                        (sxz - sxz_before)
                        + (syz - shifted_down(syz, 0.0, 0))
                        + (shifted_up(szz, 0.0, 1) - szz),
                    )
                )
            here = place + (x + row_start) * (every_column * depth)
            source = jnp.where(here == target, amplitude, 0.0)
            for c in range(3):
                first_wave = mo[s, 0, c, x] + scaled * accel[0][c]
                born = mo[s, 1, c, x] + scaled * (accel[1][c] - change * accel[0][c])
                adjoint = mo[s, 2, c, x] + scaled * accel[2][c]
                if c == 2:
                    first_wave = first_wave + scaled * source
                    adjoint = adjoint + scaled * record[s, x] * born
                accel0[s, c, x] = accel[0][c]
                mo[s, 0, c, x] = first_wave
                mo[s, 1, c, x] = born
                mo[s, 2, c, x] = adjoint
            return carry

        lax.fori_loop(0, rows, motion_row, 0, unroll=2)

    received(corners)
    for t, w in pairs:
        edge_out[0, line(slot(t, w, 0)), :] = corner_in[0, line(slot(t, w, 0)), :]
        edge_out[0, line(slot(t, w, 1)), :] = corner_in[0, line(slot(t, w, 1)), :]
        edge_out[0, line(slot(t, w, 2)), :] = corner_in[1, line(slot(t, w, 1)), :]
        edge_out[1, line(slot(t, w, 0)), :] = corner_in[1, line(slot(t, w, 0)), :]
        edge_out[1, line(slot(t, w, 1)), :] = corner_in[0, line(slot(t, w, 2)), :]
    send(edges)

    param_loads[0].wait()
    param_loads[1].wait()
    for s in range(shots):
        stress_loads[s].wait()
        motion_loads[s].wait()
        motion(s)

    low_face, up_face = (0, every), (rows - 1, every)
    left_face, right_face = (every, 0), (every, cols - 1)

    def fix_motion(s, where, c, message, at_spot, i, sign, parts=(True, True)):
        at = where + (every,)
        buoyancy = 1.0 / density[at]
        scaled = COURANT * buoyancy
        d0 = sign * message[at_spot(s, 0, i)]
        if parts[1]:
            change = density_change[at] * buoyancy
            born = scaled * (sign * message[at_spot(s, 1, i)] - change * d0)
            mo[(s, 1, c) + at] += born
        if parts[0]:
            accel0[(s, c) + at] += d0
            mo[(s, 0, c) + at] += scaled * d0
            adjoint = scaled * (sign * message[at_spot(s, 2, i)])
            if c == 2:
                adjoint = adjoint + scaled * record[(s,) + at] * born
            mo[(s, 2, c) + at] += adjoint

    side_index = lax.broadcasted_iota(jnp.int32, (rows, depth), 0)
    row_index = lax.broadcasted_iota(jnp.int32, (cols, depth), 0)

    def at_line(index, n, w, s, group, i):
        return jnp.where(index == n, edge_in[group, line(slot(s, w, i)), :], 0.0)

    def finish(s, message, at_spot, i, pushes, dst, field=None, which=(0, 1, 2)):
        scaled, change = scales(message)
        moved = {
            w: advance(scaled, change, w, message[at_spot(s, w, i)], pushes) for w in which
        }
        if field is not None:
            moved[2] = moved[2] + scaled * field * moved[1]
        for w in which:
            dst[w] = moved[w]

    def finish_left(s, cornered):
        pushes = [left_out[to_low(s, w, 0)] for w in range(waves)]
        if cornered:
            pushes = [d - at_line(side_index, 0, w, s, 1, 0) for w, d in enumerate(pushes)]
        finish(s, from_left, to_up, 2, pushes, left_halo.at[s])

    def finish_right(s, cornered):
        push_x = [-right_out[to_up(s, w, 0)] for w in range(waves)]
        push_z = [-right_out[to_up(s, w, 1)] for w in range(waves)]
        if cornered:
            push_x = [
                d + at_line(side_index, rows - 1, w, s, 0, 1) for w, d in enumerate(push_x)
            ]
            push_z = [d - at_line(side_index, 0, w, s, 0, 2) for w, d in enumerate(push_z)]
        finish(s, from_right, to_low, 1, push_x, right_halo.at[s, 0])
        finish(s, from_right, to_low, 2, push_z, right_halo.at[s, 1], record_col[s])

    def finish_low(s, which):
        pushes = [
            low_out[to_low(s, w, 0)] - at_line(row_index, 0, w, s, 1, 0) for w in range(waves)
        ]
        finish(s, from_low, to_up, 2, pushes, low_halo.at[s], None, which)

    def finish_up(s, which):
        push_y = [
            at_line(row_index, cols - 1, w, s, 0, 0) - up_out[to_up(s, w, 0)] for w in range(waves)
        ]
        finish(s, from_up, to_low, 1, push_y, up_halo.at[s, 0], None, which)
        if 0 in which:
            push_z = [
                -at_line(row_index, 0, w, s, 1, 1) - up_out[to_up(s, w, 1)] for w in range(waves)
            ]
            finish(s, from_up, to_low, 2, push_z, up_halo.at[s, 1], record_row[s])

    received(col_faces)

    @pl.when(has_up_y)
    def _():
        for s in range(shots):
            fix_motion(s, right_face, 1, from_right, to_low, 0, 1.0)
            finish_right(s, False)

    @pl.when(has_low_y)
    def _():
        for s in range(shots):
            fix_motion(s, left_face, 0, from_left, to_up, 0, -1.0)
            fix_motion(s, left_face, 2, from_left, to_up, 1, -1.0)
            finish_left(s, False)

    for copy in param_loads[2:]:
        copy.wait()

    def modulus(strain, first, second, twice):
        trace = first * (strain[0] + strain[1] + strain[2])
        return [trace + twice * strain[i] for i in range(3)] + [
            second * strain[i] for i in range(3, 6)
        ]

    def strain_of(s, w, x, lowest, highest):
        vx, vy, vz = mo[s, w, 0, x], mo[s, w, 1, x], mo[s, w, 2, x]
        vx_before = low_halo[s, w] if lowest else mo[s, w, 0, x - 1]
        vy_after = up_halo[s, 0, w] if highest else mo[s, w, 1, x + 1]
        vz_after = up_halo[s, 1, w] if highest else mo[s, w, 2, x + 1]
        vy_left = left_halo[s, w, line(x), :]
        vx_right = right_halo[s, 0, w, line(x), :]
        vz_right = right_halo[s, 1, w, line(x), :]
        return (
            vx - vx_before,
            vy - shifted_down(vy, vy_left, 0),
            vz - shifted_down(vz, 0.0, 1),
            (shifted_up(vx, vx_right, 0) - vx) + (vy_after - vy),
            (shifted_up(vx, 0.0, 1) - vx) + (vz_after - vz),
            (shifted_up(vy, 0.0, 1) - vy) + (shifted_up(vz, vz_right, 0) - vz),
        )

    def stress_row(s, x, lowest=False, highest=False, parts=(True, True)):
        first_modulus, second_modulus = lame[x], shear[x]
        twice = 2.0 * second_modulus
        e = strain_of(s, 0, x, lowest, highest)
        if parts[1]:
            second_change = shear_change[x]
            strain = strain_of(s, 1, x, lowest, highest)
            born = modulus(strain, first_modulus, second_modulus, twice)
            changed = modulus(e, lame_change[x], second_change, 2.0 * second_change)
            for c in range(6):
                st[s, 1, c, x] = st[s, 1, c, x] + COURANT * (born[c] + changed[c])
        if not parts[0]:
            return
        strain = strain_of(s, 2, x, lowest, highest)
        adjoint = modulus(strain, first_modulus, second_modulus, twice)
        a = []
        for c in range(6):
            a.append(st[s, 2, c, x] + COURANT * adjoint[c])
            st[s, 2, c, x] = a[c]
        total = (
            accel0[s, 0, x] * mo[s, 2, 0, x]
            + accel0[s, 1, x] * mo[s, 2, 1, x]
            + accel0[s, 2, x] * mo[s, 2, 2, x]
        )
        row_terms = (
            (e[0] + e[1] + e[2]) * (a[0] + a[1] + a[2]),
            2.0 * (e[0] * a[0] + e[1] * a[1] + e[2] * a[2])
            + e[3] * a[3]
            + e[4] * a[4]
            + e[5] * a[5],
            (1.0 / density[x]) * total,
        )
        for i in range(3):
            terms[i, x] = row_terms[i] if s == 0 else terms[i, x] + row_terms[i]

    for s in range(shots):

        def inner_row(x, carry, s=s):
            stress_row(s, x)
            return carry

        lax.fori_loop(1, rows - 1, inner_row, 0, unroll=2)

    received(edges)

    @pl.when(has_up_y)
    def _():
        for s in range(shots):
            finish_right(s, True)

    @pl.when(has_low_y)
    def _():
        for s in range(shots):
            finish_left(s, True)

    received(row_faces)

    @pl.when(has_up_x)
    def _():
        for s in range(shots):
            fix_motion(s, up_face, 0, from_up, to_low, 0, 1.0, (True, False))
            finish_up(s, (0, 2))

    @pl.when(has_low_x)
    def _():
        for s in range(shots):
            fix_motion(s, low_face, 1, from_low, to_up, 0, -1.0, (True, False))
            fix_motion(s, low_face, 2, from_low, to_up, 1, -1.0)
            finish_low(s, (0, 2))

    for s in range(shots):
        stress_row(s, 0, lowest=True, parts=(True, False))
        stress_row(s, rows - 1, highest=True, parts=(True, False))

    shares = []
    for k in range(1, groups):
        peer = lax.rem(me + k, groups)
        copy = pltpu.make_async_remote_copy(
            src_ref=terms.at[:, pl.ds(peer * own, own)],
            dst_ref=landed.at[k - 1],
            send_sem=share_send_sem.at[k - 1],
            recv_sem=share_recv_sem.at[k - 1],
            device_id={"shot": peer},
            device_id_type=MESH,
        )
        copy.start()
        shares.append(copy)
    received(born_faces)

    @pl.when(has_up_x)
    def _():
        for s in range(shots):
            fix_motion(s, up_face, 0, from_up, to_low, 0, 1.0, (False, True))
            finish_up(s, (1,))

    @pl.when(has_low_x)
    def _():
        for s in range(shots):
            fix_motion(s, low_face, 1, from_low, to_up, 0, -1.0, (False, True))
            finish_low(s, (1,))

    for s in range(shots):
        stress_row(s, 0, lowest=True, parts=(False, True))
        stress_row(s, rows - 1, highest=True, parts=(False, True))

    for copy in shares:
        copy.wait_recv()
    total = terms[:, pl.ds(me * own, own)]
    for k in range(1, groups):
        total = total + landed[k - 1]
    kernels[...] = total * (1.0 / total_shots)
    for copies in (row_faces, col_faces, born_faces, corners, edges):
        sent(copies)
    for copy in shares:
        copy.wait_send()


def write_kernel(st, mo, kernels_in, new_velocity, new_stress, kernels, sems):
    shots = st.shape[0]
    copies = [pltpu.make_async_copy(kernels_in, kernels, sems.at[2 * shots])]
    for s in range(shots):
        copies.append(
            pltpu.make_async_copy(st.at[s, pl.ds(1, 2)], new_stress.at[s], sems.at[2 * s])
        )
        copies.append(
            pltpu.make_async_copy(mo.at[s, pl.ds(1, 2)], new_velocity.at[s], sems.at[2 * s + 1])
        )
    for copy in copies:
        copy.start()
    for copy in copies:
        copy.wait()


def shards(
    stress_fields,
    velocity_fields,
    lame,
    shear,
    density,
    lame_change,
    shear_change,
    density_change,
    source_cell,
    source_amp,
    receiver_cell,
):
    rows, cols, depth = lame.shape
    shots, waves = stress_fields.shape[:2]
    groups = lax.axis_size("shot")
    own = rows // groups
    every_column = cols * lax.axis_size("gy")
    f32 = jnp.float32
    hbm = pl.BlockSpec(memory_space=pltpu.HBM)
    smem = pl.BlockSpec(memory_space=pltpu.SMEM)
    vmem = pl.BlockSpec(memory_space=pltpu.VMEM)
    row, col = (cols, depth), (rows, depth)
    message = shots * waves * 3 + 2
    lines = -(-shots * waves * 3 // 8) * 8
    scratch = [
        (6, rows, cols, depth),
        None,
        (shots, rows, cols, depth),
        (shots, *row),
        (shots, *col),
        (shots, 3, rows, cols, depth),
        (3, rows, cols, depth),
        (shots, waves, 6, *row),
        (shots, waves, 6, *row),
        (shots, waves, 6, *col),
        (shots, waves, 6, *col),
        (shots, waves, 2, *row),
        (shots, waves, *row),
        (2, shots, waves, *col),
        (shots, waves, *col),
        (message, *row),
        (message, *row),
        (message, *col),
        (message, *col),
        (message, *row),
        (message, *row),
        (message, *col),
        (message, *col),
        (2, lines, depth),
        (2, lines, depth),
        (2, lines, depth),
        (2, lines, depth),
        (shots, waves, *row),
        (shots, 2, waves, *row),
        (shots, waves, *col),
        (shots, 2, waves, *col),
        (max(groups - 1, 1), 3, own, cols, depth),
    ]
    scratch = [
        pltpu.VMEM(receiver_cell.shape, jnp.int32) if dims is None else pltpu.VMEM(dims, f32)
        for dims in scratch
    ]
    st, mo, kernels = pl.pallas_call(
        functools.partial(step_kernel, every_column, shots * groups),
        name="step",
        out_shape=(
            pltpu.VMEM((shots, waves, 6, rows, cols, depth), f32),
            pltpu.VMEM((shots, waves, 3, rows, cols, depth), f32),
            pltpu.VMEM((3, own, cols, depth), f32),
        ),
        in_specs=[hbm] * 9 + [smem] * 2,
        out_specs=(vmem, vmem, vmem),
        scratch_shapes=scratch
        + [
            pltpu.SemaphoreType.DMA((shots, 2)),
            pltpu.SemaphoreType.DMA((17,)),
            pltpu.SemaphoreType.DMA((7,)),
            pltpu.SemaphoreType.DMA((10,)),
            pltpu.SemaphoreType.DMA((10,)),
            pltpu.SemaphoreType.DMA((max(groups - 1, 1),)),
            pltpu.SemaphoreType.DMA((max(groups - 1, 1),)),
        ],
        compiler_params=pltpu.CompilerParams(
            collective_id=0, has_side_effects=True, vmem_limit_bytes=VMEM_LIMIT
        ),
    )(
        *(
            pltpu.with_memory_space_constraint(array, pltpu.HBM)
            for array in (
                stress_fields,
                velocity_fields,
                lame,
                shear,
                density,
                lame_change,
                shear_change,
                density_change,
                receiver_cell,
                source_cell,
                source_amp,
            )
        ),
    )
    shape = lambda *dims: jax.ShapeDtypeStruct(dims, f32)
    return pl.pallas_call(
        write_kernel,
        name="write",
        out_shape=(
            shape(shots, 2, 3, rows, cols, depth),
            shape(shots, 2, 6, rows, cols, depth),
            shape(3, own, cols, depth),
        ),
        in_specs=[vmem] * 3,
        out_specs=(hbm, hbm, hbm),
        scratch_shapes=[pltpu.SemaphoreType.DMA((2 * shots + 1,))],
        compiler_params=pltpu.CompilerParams(vmem_limit_bytes=VMEM_LIMIT),
    )(st, mo, kernels)


def solution(mesh):
    return jax.shard_map(
        shards,
        mesh=mesh,
        in_specs=(
            P("shot", None, None, "gx", "gy", None),
            P("shot", None, None, "gx", "gy", None),
            P("gx", "gy", None),
            P("gx", "gy", None),
            P("gx", "gy", None),
            P("gx", "gy", None),
            P("gx", "gy", None),
            P("gx", "gy", None),
            P("shot"),
            P("shot"),
            P("shot", None),
        ),
        out_specs=(
            P("shot", None, None, "gx", "gy", None),
            P("shot", None, None, "gx", "gy", None),
            P(None, ("gx", "shot"), "gy", None),
        ),
        check_vma=False,
    )
```

```python
import functools

import jax
import jax.numpy as jnp
from jax import lax
from jax.experimental import pallas as pl
from jax.experimental.pallas import tpu as pltpu
from jax.sharding import PartitionSpec as P

RDEPTH = 2
COURANT = 0.25
MESH = pl.DeviceIdType.MESH
VMEM_LIMIT = 32 * 1024 * 1024
RELAYED = 12


def shifted_up(tile, halo, axis):
    length = tile.shape[axis]
    index = lax.broadcasted_iota(jnp.int32, tile.shape, axis)
    return jnp.where(index == length - 1, halo, pltpu.roll(tile, length - 1, axis))


def shifted_down(tile, halo, axis):
    index = lax.broadcasted_iota(jnp.int32, tile.shape, axis)
    return jnp.where(index == 0, halo, pltpu.roll(tile, 1, axis))


def step_kernel(
    every_column,
    total_shots,
    stress,
    velocity,
    lame_in,
    shear_in,
    density_in,
    lame_change_in,
    shear_change_in,
    density_change_in,
    receivers_in,
    source_cell,
    source_amp,
    st,
    mo,
    kernels,
    params,
    receivers,
    record,
    record_row,
    record_col,
    accel0,
    terms,
    first_stress,
    last_stress,
    left_stress,
    right_stress,
    first_motion,
    last_motion,
    left_motion,
    right_motion,
    low_out,
    up_out,
    left_out,
    right_out,
    from_up,
    from_low,
    from_right,
    from_left,
    relay,
    corner_out,
    corner_in,
    edge_out,
    edge_in,
    low_halo,
    up_halo,
    left_halo,
    right_halo,
    landed,
    load_sem,
    face_sem,
    param_sem,
    send_sem,
    recv_sem,
    share_send_sem,
    share_recv_sem,
):
    shots, waves, _, rows, cols, depth = stress.shape
    gx, gy = lax.axis_index("gx"), lax.axis_index("gy")
    nx, ny = lax.axis_size("gx"), lax.axis_size("gy")
    me, groups = lax.axis_index("shot"), lax.axis_size("shot")
    own = rows // groups
    has_low_x, has_up_x = gx > 0, gx < nx - 1
    has_low_y, has_up_y = gy > 0, gy < ny - 1
    sides = (
        (has_low_x, {"gx": gx - 1}),
        (has_up_x, {"gx": gx + 1}),
        (has_low_y, {"gy": gy - 1}),
        (has_up_y, {"gy": gy + 1}),
    )
    barrier = pltpu.get_barrier_semaphore()
    for present, device in sides:

        @pl.when(present)
        def _(device=device):
            pl.semaphore_signal(barrier, inc=1, device_id=device, device_id_type=MESH)

    if nx == 4 and groups == 2:
        for mid, source in ((0, 2), (3, 1)):

            @pl.when(gx == mid)
            def _(source=source):
                pl.semaphore_signal(barrier, inc=1, device_id={"gx": source}, device_id_type=MESH)

    for k in range(1, groups):
        peer = lax.rem(me + k, groups)
        pl.semaphore_signal(barrier, inc=1, device_id={"shot": peer}, device_id_type=MESH)

    tail = 2 + shots * 7
    faces = (
        (stress.at[:, :, :, 0], first_stress),
        (stress.at[:, :, :, rows - 1], last_stress),
        (velocity.at[:, :, pl.ds(1, 2), 0], first_motion),
        (velocity.at[:, :, 0, rows - 1], last_motion),
        (density_in.at[0], low_out.at[0]),
        (density_change_in.at[0], low_out.at[1]),
        (density_in.at[rows - 1], up_out.at[0]),
        (density_change_in.at[rows - 1], up_out.at[1]),
        (stress.at[:, :, :, :, 0], left_stress),
        (stress.at[:, :, :, :, cols - 1], right_stress),
        (velocity.at[:, :, 0, :, 0], left_motion.at[0]),
        (velocity.at[:, :, 2, :, 0], left_motion.at[1]),
        (velocity.at[:, :, 1, :, cols - 1], right_motion),
        (density_in.at[:, 0], left_out.at[0]),
        (density_change_in.at[:, 0], left_out.at[1]),
        (density_in.at[:, cols - 1], right_out.at[0]),
        (density_change_in.at[:, cols - 1], right_out.at[1]),
    )
    face_loads = [
        pltpu.make_async_copy(src, dst, face_sem.at[i]) for i, (src, dst) in enumerate(faces)
    ]
    stress_loads = [
        pltpu.make_async_copy(stress.at[s], st.at[s], load_sem.at[s, 0]) for s in range(shots)
    ]
    motion_loads = [
        pltpu.make_async_copy(velocity.at[s], mo.at[s], load_sem.at[s, 1]) for s in range(shots)
    ]
    receiver_load = pltpu.make_async_copy(receivers_in, receivers, param_sem.at[6])
    sources = (density_in, density_change_in, lame_in, shear_in, lame_change_in, shear_change_in)
    param_loads = [
        pltpu.make_async_copy(source, params.at[i], param_sem.at[i])
        for i, source in enumerate(sources)
    ]
    for copy in face_loads:
        copy.start()
    receiver_load.start()
    density, density_change, lame, shear, lame_change, shear_change = (
        params.at[i] for i in range(6)
    )

    def face(src, dst, slot, device):
        return pltpu.make_async_remote_copy(
            src_ref=src,
            dst_ref=dst,
            send_sem=send_sem.at[slot],
            recv_sem=recv_sem.at[slot],
            device_id=device,
            device_id_type=MESH,
        )

    low_x, up_x, low_y, up_y = (device for _, device in sides)
    body, rest = pl.ds(0, tail), pl.ds(tail, shots * 2)
    direct = pl.ds(0, tail + shots * 2 - RELAYED)
    detour = pl.ds(tail + shots * 2 - RELAYED, RELAYED)
    relays = nx == 4 and groups == 2
    at_column = [jnp.logical_and(relays, gx == i) for i in range(4)]
    plain_low, plain_up = (
        jnp.logical_and(has_low_x, jnp.logical_not(at_column[2])),
        jnp.logical_and(has_up_x, jnp.logical_not(at_column[1])),
    )
    row_faces = (
        (face(low_out.at[body], from_up.at[body], 0, low_x), plain_low, plain_up),
        (face(up_out.at[body], from_low.at[body], 1, up_x), plain_up, plain_low),
    )
    born_faces = (
        (face(low_out.at[rest], from_up.at[rest], 8, low_x), plain_low, plain_up),
        (face(up_out.at[rest], from_low.at[rest], 9, up_x), plain_up, plain_low),
    )
    first_hops, second_hops = (), ()
    if relays:
        row_faces += (
            (face(low_out.at[direct], from_up.at[direct], 10, low_x), at_column[2], at_column[1]),
            (face(up_out.at[direct], from_low.at[direct], 11, up_x), at_column[1], at_column[2]),
        )
        first_hops = (
            (face(low_out.at[detour], relay, 12, {"gx": 0}), at_column[2], at_column[0]),
            (face(up_out.at[detour], relay, 13, {"gx": 3}), at_column[1], at_column[3]),
        )
        second_hops = (
            (face(relay, from_up.at[detour], 14, {"gx": 1}), at_column[0], at_column[1]),
            (face(relay, from_low.at[detour], 15, {"gx": 2}), at_column[3], at_column[2]),
        )
    col_faces = (
        (face(left_out, from_right, 2, low_y), has_low_y, has_up_y),
        (face(right_out, from_left, 3, up_y), has_up_y, has_low_y),
    )
    corners = (
        (face(corner_out.at[0], corner_in.at[0], 4, low_x), has_low_x, has_up_x),
        (face(corner_out.at[1], corner_in.at[1], 5, up_x), has_up_x, has_low_x),
    )
    edges = (
        (face(edge_out.at[0], edge_in.at[0], 6, low_y), has_low_y, has_up_y),
        (face(edge_out.at[1], edge_in.at[1], 7, up_y), has_up_y, has_low_y),
    )

    def send(faces):
        for copy, sends, _ in faces:

            @pl.when(sends)
            def _(copy=copy):
                copy.start()

    def sent(faces):
        for copy, sends, _ in faces:

            @pl.when(sends)
            def _(copy=copy):
                copy.wait_send()

    def received(faces):
        for copy, _, comes in faces:

            @pl.when(comes)
            def _(copy=copy):
                copy.wait_recv()

    row_start, col_start = gx * rows, gy * cols
    pairs = [(s, w) for s in range(shots) for w in range(waves)]
    every = slice(None)

    def slot(s, w, i):
        return (s * waves + w) * 3 + i

    def spot(s, w, i, early):
        if w != 1:
            return 2 + ((w // 2) * shots + s) * 3 + i
        if i == early:
            return 2 + shots * 6 + s
        return tail + s * 2 + i // (3 - early)

    def to_low(s, w, i):
        return spot(s, w, i, 2)

    def to_up(s, w, i):
        return spot(s, w, i, 1)

    def scales(message):
        buoyancy = 1.0 / message[0]
        return COURANT * buoyancy, message[1] * buoyancy

    def source_of(s, here):
        return jnp.where(here == source_cell[s], source_amp[s], 0.0)

    def advance(scaled, change, w, start, push):
        if w == 1:
            return start + scaled * (push[1] - change * push[0])
        return start + scaled * push[w]

    place = (
        lax.broadcasted_iota(jnp.int32, (cols, depth), 0) + col_start
    ) * depth + lax.broadcasted_iota(jnp.int32, (cols, depth), 1)
    side_place = (
        (lax.broadcasted_iota(jnp.int32, (rows, depth), 0) + row_start) * every_column + col_start
    ) * depth + lax.broadcasted_iota(jnp.int32, (rows, depth), 1)

    for copy in face_loads[:8]:
        copy.wait()
    low_scales, up_scales = scales(low_out), scales(up_out)
    for s in range(shots):
        push_y, push_z, push_x = [], [], []
        for w in range(waves):
            sxx, syy, szz, sxy, sxz, syz = (first_stress[s, w, i] for i in range(6))
            low_out[to_low(s, w, 0)] = sxx
            push_y.append(sxy + (shifted_up(syy, 0.0, 0) - syy) + (syz - shifted_down(syz, 0.0, 1)))
            push_z.append(sxz + (syz - shifted_down(syz, 0.0, 0)) + (shifted_up(szz, 0.0, 1) - szz))
            sxx, sxy, sxz = (last_stress[s, w, i] for i in (0, 3, 4))
            up_out[to_up(s, w, 0)] = sxy
            up_out[to_up(s, w, 1)] = sxz
            push_x.append((sxy - shifted_down(sxy, 0.0, 0)) + (sxz - shifted_down(sxz, 0.0, 1)) - sxx)
        here = place + row_start * (every_column * depth)
        for w in range(waves):
            low_out[to_low(s, w, 1)] = advance(*low_scales, w, first_motion[s, w, 0], push_y)
            moved = advance(*low_scales, w, first_motion[s, w, 1], push_z)
            if w == 0:
                moved = moved + low_scales[0] * source_of(s, here)
            low_out[to_low(s, w, 2)] = moved
            up_out[to_up(s, w, 2)] = advance(*up_scales, w, last_motion[s, w], push_x)

    for copy in face_loads[8:]:
        copy.wait()
    left_scales, right_scales = scales(left_out), scales(right_out)
    for s in range(shots):
        push_x, push_z, push_y = [], [], []
        for w in range(waves):
            sxx, syy, szz, sxy, sxz, syz = (left_stress[s, w, i] for i in range(6))
            left_out[to_low(s, w, 0)] = syy
            push_x.append((shifted_up(sxx, 0.0, 0) - sxx) + sxy + (sxz - shifted_down(sxz, 0.0, 1)))
            push_z.append((sxz - shifted_down(sxz, 0.0, 0)) + syz + (shifted_up(szz, 0.0, 1) - szz))
            syy, sxy, syz = (right_stress[s, w, i] for i in (1, 3, 5))
            right_out[to_up(s, w, 0)] = sxy
            right_out[to_up(s, w, 1)] = syz
            push_y.append((sxy - shifted_down(sxy, 0.0, 0)) + (syz - shifted_down(syz, 0.0, 1)) - syy)
        for w in range(waves):
            left_out[to_low(s, w, 1)] = advance(*left_scales, w, left_motion[0, s, w], push_x)
            moved = advance(*left_scales, w, left_motion[1, s, w], push_z)
            if w == 0:
                moved = moved + left_scales[0] * source_of(s, side_place)
            left_out[to_low(s, w, 2)] = moved
            right_out[to_up(s, w, 2)] = advance(*right_scales, w, right_motion[s, w], push_y)

    def line(n):
        return pl.ds(n, 1)

    first, last = line(0), line(cols - 1)
    for s, w in pairs:
        corner_out[0, line(slot(s, w, 0)), :] = first_stress[s, w, 1, first, :]
        corner_out[0, line(slot(s, w, 1)), :] = first_stress[s, w, 0, first, :]
        corner_out[0, line(slot(s, w, 2)), :] = first_stress[s, w, 5, last, :]
        corner_out[1, line(slot(s, w, 0)), :] = last_stress[s, w, 3, last, :]
        corner_out[1, line(slot(s, w, 1)), :] = last_stress[s, w, 4, first, :]

    neighbours = groups - 1
    for present, _ in sides:
        neighbours = neighbours + present.astype(jnp.int32)
    if relays:
        neighbours = neighbours + jnp.logical_or(gx == 1, gx == 2).astype(jnp.int32)
    pl.semaphore_wait(barrier, neighbours)
    send(corners)
    send(first_hops)
    send(row_faces)
    send(col_faces)
    send(born_faces)
    param_loads[0].start()
    param_loads[1].start()
    for s in range(shots):
        stress_loads[s].start()
        motion_loads[s].start()
    for copy in param_loads[2:]:
        copy.start()

    for comes, ref in (
        (has_up_x, corner_in.at[0]),
        (has_low_x, corner_in.at[1]),
        (has_up_y, edge_in.at[0]),
        (has_low_y, edge_in.at[1]),
        (has_up_x, up_halo),
        (has_low_x, low_halo),
        (has_up_y, right_halo),
        (has_low_y, left_halo),
    ):

        @pl.when(jnp.logical_not(comes))
        def _(ref=ref):
            ref[...] = jnp.zeros(ref.shape, jnp.float32)

    receiver_load.wait()
    count = receivers.shape[1]
    plane = (lax.broadcasted_iota(jnp.int32, (count, depth), 1) == RDEPTH).astype(jnp.bfloat16)

    def count_at(s, cell):
        marks = jnp.where(receivers[pl.ds(s, 1), :] == cell, 1.0, 0.0).astype(jnp.bfloat16)
        return jnp.dot(marks, plane, preferred_element_type=jnp.float32)

    cell = (
        lax.broadcasted_iota(jnp.int32, (rows, cols, count), 0) + row_start
    ) * every_column + (lax.broadcasted_iota(jnp.int32, (rows, cols, count), 1) + col_start)
    cell = cell.reshape(rows * cols, count)
    next_row = (row_start + rows) * every_column + (
        lax.broadcasted_iota(jnp.int32, (cols, count), 0) + col_start
    )
    next_col = (lax.broadcasted_iota(jnp.int32, (rows, count), 0) + row_start) * every_column + (
        col_start + cols
    )
    for s in range(shots):
        record[s] = count_at(s, cell).reshape(rows, cols, depth)
        record_row[s] = count_at(s, next_row)
        record_col[s] = count_at(s, next_col)

    def motion(s):
        target, amplitude = source_cell[s], source_amp[s]

        def motion_row(x, carry):
            after = lax.rem(x + 1, rows)
            before = lax.rem(x + rows - 1, rows)
            last, first = x == rows - 1, x == 0
            buoyancy = 1.0 / density[x]
            scaled = COURANT * buoyancy
            change = density_change[x] * buoyancy
            accel = []
            for w in range(waves):
                sxx, syy, szz = st[s, w, 0, x], st[s, w, 1, x], st[s, w, 2, x]
                sxy, sxz, syz = st[s, w, 3, x], st[s, w, 4, x], st[s, w, 5, x]
                sxx_after = jnp.where(last, 0.0, st[s, w, 0, after])
                sxy_before = jnp.where(first, 0.0, st[s, w, 3, before])
                sxz_before = jnp.where(first, 0.0, st[s, w, 4, before])
                accel.append(
                    (
                        (sxx_after - sxx)
                        + (sxy - shifted_down(sxy, 0.0, 0))
                        + (sxz - shifted_down(sxz, 0.0, 1)),
                        (sxy - sxy_before)
                        + (shifted_up(syy, 0.0, 0) - syy)
                        + (syz - shifted_down(syz, 0.0, 1)),
                        (sxz - sxz_before)
                        + (syz - shifted_down(syz, 0.0, 0))
                        + (shifted_up(szz, 0.0, 1) - szz),
                    )
                )
            here = place + (x + row_start) * (every_column * depth)
            source = jnp.where(here == target, amplitude, 0.0)
            for c in range(3):
                first_wave = mo[s, 0, c, x] + scaled * accel[0][c]
                born = mo[s, 1, c, x] + scaled * (accel[1][c] - change * accel[0][c])
                adjoint = mo[s, 2, c, x] + scaled * accel[2][c]
                if c == 2:
                    first_wave = first_wave + scaled * source
                    adjoint = adjoint + scaled * record[s, x] * born
                accel0[s, c, x] = accel[0][c]
                mo[s, 0, c, x] = first_wave
                mo[s, 1, c, x] = born
                mo[s, 2, c, x] = adjoint
            return carry

        lax.fori_loop(0, rows, motion_row, 0, unroll=2)

    received(corners)
    for t, w in pairs:
        edge_out[0, line(slot(t, w, 0)), :] = corner_in[0, line(slot(t, w, 0)), :]
        edge_out[0, line(slot(t, w, 1)), :] = corner_in[0, line(slot(t, w, 1)), :]
        edge_out[0, line(slot(t, w, 2)), :] = corner_in[1, line(slot(t, w, 1)), :]
        edge_out[1, line(slot(t, w, 0)), :] = corner_in[1, line(slot(t, w, 0)), :]
        edge_out[1, line(slot(t, w, 1)), :] = corner_in[0, line(slot(t, w, 2)), :]
    send(edges)

    param_loads[0].wait()
    param_loads[1].wait()
    for s in range(shots):
        stress_loads[s].wait()
        motion_loads[s].wait()
        motion(s)
        if s == 0:
            received(first_hops)
            send(second_hops)

    low_face, up_face = (0, every), (rows - 1, every)
    left_face, right_face = (every, 0), (every, cols - 1)

    def fix_motion(s, where, c, message, at_spot, i, sign, parts=(True, True)):
        at = where + (every,)
        buoyancy = 1.0 / density[at]
        scaled = COURANT * buoyancy
        d0 = sign * message[at_spot(s, 0, i)]
        if parts[1]:
            change = density_change[at] * buoyancy
            born = scaled * (sign * message[at_spot(s, 1, i)] - change * d0)
            mo[(s, 1, c) + at] += born
        if parts[0]:
            accel0[(s, c) + at] += d0
            mo[(s, 0, c) + at] += scaled * d0
            adjoint = scaled * (sign * message[at_spot(s, 2, i)])
            if c == 2:
                adjoint = adjoint + scaled * record[(s,) + at] * born
            mo[(s, 2, c) + at] += adjoint

    side_index = lax.broadcasted_iota(jnp.int32, (rows, depth), 0)
    row_index = lax.broadcasted_iota(jnp.int32, (cols, depth), 0)

    def at_line(index, n, w, s, group, i):
        return jnp.where(index == n, edge_in[group, line(slot(s, w, i)), :], 0.0)

    def finish(s, message, at_spot, i, pushes, dst, field=None, which=(0, 1, 2)):
        scaled, change = scales(message)
        moved = {
            w: advance(scaled, change, w, message[at_spot(s, w, i)], pushes) for w in which
        }
        if field is not None:
            moved[2] = moved[2] + scaled * field * moved[1]
        for w in which:
            dst[w] = moved[w]

    def finish_left(s, cornered):
        pushes = [left_out[to_low(s, w, 0)] for w in range(waves)]
        if cornered:
            pushes = [d - at_line(side_index, 0, w, s, 1, 0) for w, d in enumerate(pushes)]
        finish(s, from_left, to_up, 2, pushes, left_halo.at[s])

    def finish_right(s, cornered):
        push_x = [-right_out[to_up(s, w, 0)] for w in range(waves)]
        push_z = [-right_out[to_up(s, w, 1)] for w in range(waves)]
        if cornered:
            push_x = [
                d + at_line(side_index, rows - 1, w, s, 0, 1) for w, d in enumerate(push_x)
            ]
            push_z = [d - at_line(side_index, 0, w, s, 0, 2) for w, d in enumerate(push_z)]
        finish(s, from_right, to_low, 1, push_x, right_halo.at[s, 0])
        finish(s, from_right, to_low, 2, push_z, right_halo.at[s, 1], record_col[s])

    def finish_low(s, which):
        pushes = [
            low_out[to_low(s, w, 0)] - at_line(row_index, 0, w, s, 1, 0) for w in range(waves)
        ]
        finish(s, from_low, to_up, 2, pushes, low_halo.at[s], None, which)

    def finish_up(s, which):
        push_y = [
            at_line(row_index, cols - 1, w, s, 0, 0) - up_out[to_up(s, w, 0)] for w in range(waves)
        ]
        finish(s, from_up, to_low, 1, push_y, up_halo.at[s, 0], None, which)
        if 0 in which:
            push_z = [
                -at_line(row_index, 0, w, s, 1, 1) - up_out[to_up(s, w, 1)] for w in range(waves)
            ]
            finish(s, from_up, to_low, 2, push_z, up_halo.at[s, 1], record_row[s])

    received(col_faces)

    @pl.when(has_up_y)
    def _():
        for s in range(shots):
            fix_motion(s, right_face, 1, from_right, to_low, 0, 1.0)
            finish_right(s, False)

    @pl.when(has_low_y)
    def _():
        for s in range(shots):
            fix_motion(s, left_face, 0, from_left, to_up, 0, -1.0)
            fix_motion(s, left_face, 2, from_left, to_up, 1, -1.0)
            finish_left(s, False)

    for copy in param_loads[2:]:
        copy.wait()

    def modulus(strain, first, second, twice):
        trace = first * (strain[0] + strain[1] + strain[2])
        return [trace + twice * strain[i] for i in range(3)] + [
            second * strain[i] for i in range(3, 6)
        ]

    def strain_of(s, w, x, lowest, highest):
        vx, vy, vz = mo[s, w, 0, x], mo[s, w, 1, x], mo[s, w, 2, x]
        vx_before = low_halo[s, w] if lowest else mo[s, w, 0, x - 1]
        vy_after = up_halo[s, 0, w] if highest else mo[s, w, 1, x + 1]
        vz_after = up_halo[s, 1, w] if highest else mo[s, w, 2, x + 1]
        vy_left = left_halo[s, w, line(x), :]
        vx_right = right_halo[s, 0, w, line(x), :]
        vz_right = right_halo[s, 1, w, line(x), :]
        return (
            vx - vx_before,
            vy - shifted_down(vy, vy_left, 0),
            vz - shifted_down(vz, 0.0, 1),
            (shifted_up(vx, vx_right, 0) - vx) + (vy_after - vy),
            (shifted_up(vx, 0.0, 1) - vx) + (vz_after - vz),
            (shifted_up(vy, 0.0, 1) - vy) + (shifted_up(vz, vz_right, 0) - vz),
        )

    def stress_row(s, x, lowest=False, highest=False, parts=(True, True)):
        first_modulus, second_modulus = lame[x], shear[x]
        twice = 2.0 * second_modulus
        e = strain_of(s, 0, x, lowest, highest)
        if parts[1]:
            second_change = shear_change[x]
            strain = strain_of(s, 1, x, lowest, highest)
            born = modulus(strain, first_modulus, second_modulus, twice)
            changed = modulus(e, lame_change[x], second_change, 2.0 * second_change)
            for c in range(6):
                st[s, 1, c, x] = st[s, 1, c, x] + COURANT * (born[c] + changed[c])
        if not parts[0]:
            return
        strain = strain_of(s, 2, x, lowest, highest)
        adjoint = modulus(strain, first_modulus, second_modulus, twice)
        a = []
        for c in range(6):
            a.append(st[s, 2, c, x] + COURANT * adjoint[c])
            st[s, 2, c, x] = a[c]
        total = (
            accel0[s, 0, x] * mo[s, 2, 0, x]
            + accel0[s, 1, x] * mo[s, 2, 1, x]
            + accel0[s, 2, x] * mo[s, 2, 2, x]
        )
        row_terms = (
            (e[0] + e[1] + e[2]) * (a[0] + a[1] + a[2]),
            2.0 * (e[0] * a[0] + e[1] * a[1] + e[2] * a[2])
            + e[3] * a[3]
            + e[4] * a[4]
            + e[5] * a[5],
            (1.0 / density[x]) * total,
        )
        for i in range(3):
            terms[i, x] = row_terms[i] if s == 0 else terms[i, x] + row_terms[i]

    for s in range(shots):

        def inner_row(x, carry, s=s):
            stress_row(s, x)
            return carry

        lax.fori_loop(1, rows - 1, inner_row, 0, unroll=rows - 2)

    received(edges)

    @pl.when(has_up_y)
    def _():
        for s in range(shots):
            finish_right(s, True)

    @pl.when(has_low_y)
    def _():
        for s in range(shots):
            finish_left(s, True)

    received(row_faces)
    received(second_hops)

    @pl.when(has_up_x)
    def _():
        for s in range(shots):
            fix_motion(s, up_face, 0, from_up, to_low, 0, 1.0, (True, False))
            finish_up(s, (0, 2))

    @pl.when(has_low_x)
    def _():
        for s in range(shots):
            fix_motion(s, low_face, 1, from_low, to_up, 0, -1.0, (True, False))
            fix_motion(s, low_face, 2, from_low, to_up, 1, -1.0)
            finish_low(s, (0, 2))

    for s in range(shots):
        stress_row(s, 0, lowest=True, parts=(True, False))
        stress_row(s, rows - 1, highest=True, parts=(True, False))

    shares = []
    for k in range(1, groups):
        peer = lax.rem(me + k, groups)
        copy = pltpu.make_async_remote_copy(
            src_ref=terms.at[:, pl.ds(peer * own, own)],
            dst_ref=landed.at[k - 1],
            send_sem=share_send_sem.at[k - 1],
            recv_sem=share_recv_sem.at[k - 1],
            device_id={"shot": peer},
            device_id_type=MESH,
        )
        copy.start()
        shares.append(copy)
    received(born_faces)

    @pl.when(has_up_x)
    def _():
        for s in range(shots):
            fix_motion(s, up_face, 0, from_up, to_low, 0, 1.0, (False, True))
            finish_up(s, (1,))

    @pl.when(has_low_x)
    def _():
        for s in range(shots):
            fix_motion(s, low_face, 1, from_low, to_up, 0, -1.0, (False, True))
            finish_low(s, (1,))

    for s in range(shots):
        stress_row(s, 0, lowest=True, parts=(False, True))
        stress_row(s, rows - 1, highest=True, parts=(False, True))

    for copy in shares:
        copy.wait_recv()
    total = terms[:, pl.ds(me * own, own)]
    for k in range(1, groups):
        total = total + landed[k - 1]
    kernels[...] = total * (1.0 / total_shots)
    for copies in (row_faces, col_faces, born_faces, corners, edges, first_hops, second_hops):
        sent(copies)
    for copy in shares:
        copy.wait_send()


def write_kernel(st, mo, kernels_in, new_velocity, new_stress, kernels, sems):
    shots = st.shape[0]
    copies = [pltpu.make_async_copy(kernels_in, kernels, sems.at[2 * shots])]
    for s in range(shots):
        copies.append(
            pltpu.make_async_copy(st.at[s, pl.ds(1, 2)], new_stress.at[s], sems.at[2 * s])
        )
        copies.append(
            pltpu.make_async_copy(mo.at[s, pl.ds(1, 2)], new_velocity.at[s], sems.at[2 * s + 1])
        )
    for copy in copies:
        copy.start()
    for copy in copies:
        copy.wait()


def shards(
    stress_fields,
    velocity_fields,
    lame,
    shear,
    density,
    lame_change,
    shear_change,
    density_change,
    source_cell,
    source_amp,
    receiver_cell,
):
    rows, cols, depth = lame.shape
    shots, waves = stress_fields.shape[:2]
    groups = lax.axis_size("shot")
    own = rows // groups
    every_column = cols * lax.axis_size("gy")
    f32 = jnp.float32
    hbm = pl.BlockSpec(memory_space=pltpu.HBM)
    smem = pl.BlockSpec(memory_space=pltpu.SMEM)
    vmem = pl.BlockSpec(memory_space=pltpu.VMEM)
    row, col = (cols, depth), (rows, depth)
    message = shots * waves * 3 + 2
    lines = -(-shots * waves * 3 // 8) * 8
    scratch = [
        (6, rows, cols, depth),
        None,
        (shots, rows, cols, depth),
        (shots, *row),
        (shots, *col),
        (shots, 3, rows, cols, depth),
        (3, rows, cols, depth),
        (shots, waves, 6, *row),
        (shots, waves, 6, *row),
        (shots, waves, 6, *col),
        (shots, waves, 6, *col),
        (shots, waves, 2, *row),
        (shots, waves, *row),
        (2, shots, waves, *col),
        (shots, waves, *col),
        (message, *row),
        (message, *row),
        (message, *col),
        (message, *col),
        (message, *row),
        (message, *row),
        (message, *col),
        (message, *col),
        (RELAYED, *row),
        (2, lines, depth),
        (2, lines, depth),
        (2, lines, depth),
        (2, lines, depth),
        (shots, waves, *row),
        (shots, 2, waves, *row),
        (shots, waves, *col),
        (shots, 2, waves, *col),
        (max(groups - 1, 1), 3, own, cols, depth),
    ]
    scratch = [
        pltpu.VMEM(receiver_cell.shape, jnp.int32) if dims is None else pltpu.VMEM(dims, f32)
        for dims in scratch
    ]
    st, mo, kernels = pl.pallas_call(
        functools.partial(step_kernel, every_column, shots * groups),
        name="step",
        out_shape=(
            pltpu.VMEM((shots, waves, 6, rows, cols, depth), f32),
            pltpu.VMEM((shots, waves, 3, rows, cols, depth), f32),
            pltpu.VMEM((3, own, cols, depth), f32),
        ),
        in_specs=[hbm] * 9 + [smem] * 2,
        out_specs=(vmem, vmem, vmem),
        scratch_shapes=scratch
        + [
            pltpu.SemaphoreType.DMA((shots, 2)),
            pltpu.SemaphoreType.DMA((17,)),
            pltpu.SemaphoreType.DMA((7,)),
            pltpu.SemaphoreType.DMA((16,)),
            pltpu.SemaphoreType.DMA((16,)),
            pltpu.SemaphoreType.DMA((max(groups - 1, 1),)),
            pltpu.SemaphoreType.DMA((max(groups - 1, 1),)),
        ],
        compiler_params=pltpu.CompilerParams(
            collective_id=0, has_side_effects=True, vmem_limit_bytes=VMEM_LIMIT
        ),
    )(
        *(
            pltpu.with_memory_space_constraint(array, pltpu.HBM)
            for array in (
                stress_fields,
                velocity_fields,
                lame,
                shear,
                density,
                lame_change,
                shear_change,
                density_change,
                receiver_cell,
                source_cell,
                source_amp,
            )
        ),
    )
    shape = lambda *dims: jax.ShapeDtypeStruct(dims, f32)
    return pl.pallas_call(
        write_kernel,
        name="write",
        out_shape=(
            shape(shots, 2, 3, rows, cols, depth),
            shape(shots, 2, 6, rows, cols, depth),
            shape(3, own, cols, depth),
        ),
        in_specs=[vmem] * 3,
        out_specs=(hbm, hbm, hbm),
        scratch_shapes=[pltpu.SemaphoreType.DMA((2 * shots + 1,))],
        compiler_params=pltpu.CompilerParams(vmem_limit_bytes=VMEM_LIMIT),
    )(st, mo, kernels)


def solution(mesh):
    return jax.shard_map(
        shards,
        mesh=mesh,
        in_specs=(
            P("shot", None, None, "gx", "gy", None),
            P("shot", None, None, "gx", "gy", None),
            P("gx", "gy", None),
            P("gx", "gy", None),
            P("gx", "gy", None),
            P("gx", "gy", None),
            P("gx", "gy", None),
            P("gx", "gy", None),
            P("shot"),
            P("shot"),
            P("shot", None),
        ),
        out_specs=(
            P("shot", None, None, "gx", "gy", None),
            P("shot", None, None, "gx", "gy", None),
            P(None, ("gx", "shot"), "gy", None),
        ),
        check_vma=False,
    )
```

```python
import functools

import jax
import jax.numpy as jnp
from jax import lax
from jax.experimental import pallas as pl
from jax.experimental.pallas import tpu as pltpu
from jax.sharding import PartitionSpec as P

RDEPTH = 2
COURANT = 0.25
MESH = pl.DeviceIdType.MESH
VMEM_LIMIT = 32 * 1024 * 1024
RELAYED = 12


def shifted_up(tile, halo, axis):
    length = tile.shape[axis]
    index = lax.broadcasted_iota(jnp.int32, tile.shape, axis)
    return jnp.where(index == length - 1, halo, pltpu.roll(tile, length - 1, axis))


def shifted_down(tile, halo, axis):
    index = lax.broadcasted_iota(jnp.int32, tile.shape, axis)
    return jnp.where(index == 0, halo, pltpu.roll(tile, 1, axis))


def step_kernel(
    every_column,
    total_shots,
    stress,
    velocity,
    lame_in,
    shear_in,
    density_in,
    lame_change_in,
    shear_change_in,
    density_change_in,
    receivers_in,
    source_cell,
    source_amp,
    st,
    mo,
    kernels,
    params,
    receivers,
    record,
    record_row,
    record_col,
    accel0,
    terms,
    first_stress,
    last_stress,
    left_stress,
    right_stress,
    first_motion,
    last_motion,
    left_motion,
    right_motion,
    low_out,
    up_out,
    left_out,
    right_out,
    from_up,
    from_low,
    from_right,
    from_left,
    relay,
    corner_out,
    corner_in,
    edge_out,
    edge_in,
    low_halo,
    up_halo,
    left_halo,
    right_halo,
    edge_terms,
    landed,
    landed_edge,
    load_sem,
    face_sem,
    param_sem,
    send_sem,
    recv_sem,
    share_send_sem,
    share_recv_sem,
):
    shots, waves, _, rows, cols, depth = stress.shape
    gx, gy = lax.axis_index("gx"), lax.axis_index("gy")
    nx, ny = lax.axis_size("gx"), lax.axis_size("gy")
    me, groups = lax.axis_index("shot"), lax.axis_size("shot")
    own = rows // groups
    has_low_x, has_up_x = gx > 0, gx < nx - 1
    has_low_y, has_up_y = gy > 0, gy < ny - 1
    sides = (
        (has_low_x, {"gx": gx - 1}),
        (has_up_x, {"gx": gx + 1}),
        (has_low_y, {"gy": gy - 1}),
        (has_up_y, {"gy": gy + 1}),
    )
    barrier = pltpu.get_barrier_semaphore()
    for present, device in sides:

        @pl.when(present)
        def _(device=device):
            pl.semaphore_signal(barrier, inc=1, device_id=device, device_id_type=MESH)

    if nx == 4 and groups == 2:
        for mid, source in ((0, 2), (3, 1)):

            @pl.when(gx == mid)
            def _(source=source):
                pl.semaphore_signal(barrier, inc=1, device_id={"gx": source}, device_id_type=MESH)

    for k in range(1, groups):
        peer = lax.rem(me + k, groups)
        pl.semaphore_signal(barrier, inc=1, device_id={"shot": peer}, device_id_type=MESH)

    tail = 2 + shots * 7
    faces = (
        (stress.at[:, :, :, 0], first_stress),
        (stress.at[:, :, :, rows - 1], last_stress),
        (velocity.at[:, :, pl.ds(1, 2), 0], first_motion),
        (velocity.at[:, :, 0, rows - 1], last_motion),
        (density_in.at[0], low_out.at[0]),
        (density_change_in.at[0], low_out.at[1]),
        (density_in.at[rows - 1], up_out.at[0]),
        (density_change_in.at[rows - 1], up_out.at[1]),
        (stress.at[:, :, :, :, 0], left_stress),
        (stress.at[:, :, :, :, cols - 1], right_stress),
        (velocity.at[:, :, 0, :, 0], left_motion.at[0]),
        (velocity.at[:, :, 2, :, 0], left_motion.at[1]),
        (velocity.at[:, :, 1, :, cols - 1], right_motion),
        (density_in.at[:, 0], left_out.at[0]),
        (density_change_in.at[:, 0], left_out.at[1]),
        (density_in.at[:, cols - 1], right_out.at[0]),
        (density_change_in.at[:, cols - 1], right_out.at[1]),
    )
    face_loads = [
        pltpu.make_async_copy(src, dst, face_sem.at[i]) for i, (src, dst) in enumerate(faces)
    ]
    stress_loads = [
        pltpu.make_async_copy(stress.at[s], st.at[s], load_sem.at[s, 0]) for s in range(shots)
    ]
    motion_loads = [
        pltpu.make_async_copy(velocity.at[s], mo.at[s], load_sem.at[s, 1]) for s in range(shots)
    ]
    receiver_load = pltpu.make_async_copy(receivers_in, receivers, param_sem.at[6])
    sources = (density_in, density_change_in, lame_in, shear_in, lame_change_in, shear_change_in)
    param_loads = [
        pltpu.make_async_copy(source, params.at[i], param_sem.at[i])
        for i, source in enumerate(sources)
    ]
    for copy in face_loads:
        copy.start()
    receiver_load.start()
    density, density_change, lame, shear, lame_change, shear_change = (
        params.at[i] for i in range(6)
    )

    def face(src, dst, slot, device):
        return pltpu.make_async_remote_copy(
            src_ref=src,
            dst_ref=dst,
            send_sem=send_sem.at[slot],
            recv_sem=recv_sem.at[slot],
            device_id=device,
            device_id_type=MESH,
        )

    low_x, up_x, low_y, up_y = (device for _, device in sides)
    body, rest = pl.ds(0, tail), pl.ds(tail, shots * 2)
    direct = pl.ds(0, tail + shots * 2 - RELAYED)
    detour = pl.ds(tail + shots * 2 - RELAYED, RELAYED)
    relays = nx == 4 and groups == 2
    at_column = [jnp.logical_and(relays, gx == i) for i in range(4)]
    plain_low, plain_up = (
        jnp.logical_and(has_low_x, jnp.logical_not(at_column[2])),
        jnp.logical_and(has_up_x, jnp.logical_not(at_column[1])),
    )
    row_faces = (
        (face(low_out.at[body], from_up.at[body], 0, low_x), plain_low, plain_up),
        (face(up_out.at[body], from_low.at[body], 1, up_x), plain_up, plain_low),
    )
    born_faces = (
        (face(low_out.at[rest], from_up.at[rest], 8, low_x), plain_low, plain_up),
        (face(up_out.at[rest], from_low.at[rest], 9, up_x), plain_up, plain_low),
    )
    first_hops, second_hops = (), ()
    if relays:
        row_faces += (
            (face(low_out.at[direct], from_up.at[direct], 10, low_x), at_column[2], at_column[1]),
            (face(up_out.at[direct], from_low.at[direct], 11, up_x), at_column[1], at_column[2]),
        )
        first_hops = (
            (face(low_out.at[detour], relay, 12, {"gx": 0}), at_column[2], at_column[0]),
            (face(up_out.at[detour], relay, 13, {"gx": 3}), at_column[1], at_column[3]),
        )
        second_hops = (
            (face(relay, from_up.at[detour], 14, {"gx": 1}), at_column[0], at_column[1]),
            (face(relay, from_low.at[detour], 15, {"gx": 2}), at_column[3], at_column[2]),
        )
    col_faces = (
        (face(left_out, from_right, 2, low_y), has_low_y, has_up_y),
        (face(right_out, from_left, 3, up_y), has_up_y, has_low_y),
    )
    corners = (
        (face(corner_out.at[0], corner_in.at[0], 4, low_x), has_low_x, has_up_x),
        (face(corner_out.at[1], corner_in.at[1], 5, up_x), has_up_x, has_low_x),
    )
    edges = (
        (face(edge_out.at[0], edge_in.at[0], 6, low_y), has_low_y, has_up_y),
        (face(edge_out.at[1], edge_in.at[1], 7, up_y), has_up_y, has_low_y),
    )

    def send(faces):
        for copy, sends, _ in faces:

            @pl.when(sends)
            def _(copy=copy):
                copy.start()

    def sent(faces):
        for copy, sends, _ in faces:

            @pl.when(sends)
            def _(copy=copy):
                copy.wait_send()

    def received(faces):
        for copy, _, comes in faces:

            @pl.when(comes)
            def _(copy=copy):
                copy.wait_recv()

    row_start, col_start = gx * rows, gy * cols
    pairs = [(s, w) for s in range(shots) for w in range(waves)]
    every = slice(None)

    def slot(s, w, i):
        return (s * waves + w) * 3 + i

    def spot(s, w, i, early):
        if w != 1:
            return 2 + ((w // 2) * shots + s) * 3 + i
        if i == early:
            return 2 + shots * 6 + s
        return tail + s * 2 + i // (3 - early)

    def to_low(s, w, i):
        return spot(s, w, i, 2)

    def to_up(s, w, i):
        return spot(s, w, i, 1)

    def scales(message):
        buoyancy = 1.0 / message[0]
        return COURANT * buoyancy, message[1] * buoyancy

    def source_of(s, here):
        return jnp.where(here == source_cell[s], source_amp[s], 0.0)

    def advance(scaled, change, w, start, push):
        if w == 1:
            return start + scaled * (push[1] - change * push[0])
        return start + scaled * push[w]

    place = (
        lax.broadcasted_iota(jnp.int32, (cols, depth), 0) + col_start
    ) * depth + lax.broadcasted_iota(jnp.int32, (cols, depth), 1)
    side_place = (
        (lax.broadcasted_iota(jnp.int32, (rows, depth), 0) + row_start) * every_column + col_start
    ) * depth + lax.broadcasted_iota(jnp.int32, (rows, depth), 1)

    for copy in face_loads[:8]:
        copy.wait()
    low_scales, up_scales = scales(low_out), scales(up_out)
    for s in range(shots):
        push_y, push_z, push_x = [], [], []
        for w in range(waves):
            sxx, syy, szz, sxy, sxz, syz = (first_stress[s, w, i] for i in range(6))
            low_out[to_low(s, w, 0)] = sxx
            push_y.append(sxy + (shifted_up(syy, 0.0, 0) - syy) + (syz - shifted_down(syz, 0.0, 1)))
            push_z.append(sxz + (syz - shifted_down(syz, 0.0, 0)) + (shifted_up(szz, 0.0, 1) - szz))
            sxx, sxy, sxz = (last_stress[s, w, i] for i in (0, 3, 4))
            up_out[to_up(s, w, 0)] = sxy
            up_out[to_up(s, w, 1)] = sxz
            push_x.append((sxy - shifted_down(sxy, 0.0, 0)) + (sxz - shifted_down(sxz, 0.0, 1)) - sxx)
        here = place + row_start * (every_column * depth)
        for w in range(waves):
            low_out[to_low(s, w, 1)] = advance(*low_scales, w, first_motion[s, w, 0], push_y)
            moved = advance(*low_scales, w, first_motion[s, w, 1], push_z)
            if w == 0:
                moved = moved + low_scales[0] * source_of(s, here)
            low_out[to_low(s, w, 2)] = moved
            up_out[to_up(s, w, 2)] = advance(*up_scales, w, last_motion[s, w], push_x)

    for copy in face_loads[8:]:
        copy.wait()
    left_scales, right_scales = scales(left_out), scales(right_out)
    for s in range(shots):
        push_x, push_z, push_y = [], [], []
        for w in range(waves):
            sxx, syy, szz, sxy, sxz, syz = (left_stress[s, w, i] for i in range(6))
            left_out[to_low(s, w, 0)] = syy
            push_x.append((shifted_up(sxx, 0.0, 0) - sxx) + sxy + (sxz - shifted_down(sxz, 0.0, 1)))
            push_z.append((sxz - shifted_down(sxz, 0.0, 0)) + syz + (shifted_up(szz, 0.0, 1) - szz))
            syy, sxy, syz = (right_stress[s, w, i] for i in (1, 3, 5))
            right_out[to_up(s, w, 0)] = sxy
            right_out[to_up(s, w, 1)] = syz
            push_y.append((sxy - shifted_down(sxy, 0.0, 0)) + (syz - shifted_down(syz, 0.0, 1)) - syy)
        for w in range(waves):
            left_out[to_low(s, w, 1)] = advance(*left_scales, w, left_motion[0, s, w], push_x)
            moved = advance(*left_scales, w, left_motion[1, s, w], push_z)
            if w == 0:
                moved = moved + left_scales[0] * source_of(s, side_place)
            left_out[to_low(s, w, 2)] = moved
            right_out[to_up(s, w, 2)] = advance(*right_scales, w, right_motion[s, w], push_y)

    def line(n):
        return pl.ds(n, 1)

    first, last = line(0), line(cols - 1)
    for s, w in pairs:
        corner_out[0, line(slot(s, w, 0)), :] = first_stress[s, w, 1, first, :]
        corner_out[0, line(slot(s, w, 1)), :] = first_stress[s, w, 0, first, :]
        corner_out[0, line(slot(s, w, 2)), :] = first_stress[s, w, 5, last, :]
        corner_out[1, line(slot(s, w, 0)), :] = last_stress[s, w, 3, last, :]
        corner_out[1, line(slot(s, w, 1)), :] = last_stress[s, w, 4, first, :]

    neighbours = groups - 1
    for present, _ in sides:
        neighbours = neighbours + present.astype(jnp.int32)
    if relays:
        neighbours = neighbours + jnp.logical_or(gx == 1, gx == 2).astype(jnp.int32)
    pl.semaphore_wait(barrier, neighbours)
    send(corners)
    send(first_hops)
    send(row_faces)
    send(col_faces)
    send(born_faces)
    param_loads[0].start()
    param_loads[1].start()
    for s in range(shots):
        stress_loads[s].start()
        motion_loads[s].start()
    for copy in param_loads[2:]:
        copy.start()

    for comes, ref in (
        (has_up_x, corner_in.at[0]),
        (has_low_x, corner_in.at[1]),
        (has_up_y, edge_in.at[0]),
        (has_low_y, edge_in.at[1]),
        (has_up_x, up_halo),
        (has_low_x, low_halo),
        (has_up_y, right_halo),
        (has_low_y, left_halo),
    ):

        @pl.when(jnp.logical_not(comes))
        def _(ref=ref):
            ref[...] = jnp.zeros(ref.shape, jnp.float32)

    for x in (0, rows - 1):
        terms[:, x] = jnp.zeros((3, cols, depth), jnp.float32)

    receiver_load.wait()
    count = receivers.shape[1]
    plane = (lax.broadcasted_iota(jnp.int32, (count, depth), 1) == RDEPTH).astype(jnp.bfloat16)

    def count_at(s, cell):
        marks = jnp.where(receivers[pl.ds(s, 1), :] == cell, 1.0, 0.0).astype(jnp.bfloat16)
        return jnp.dot(marks, plane, preferred_element_type=jnp.float32)

    cell = (
        lax.broadcasted_iota(jnp.int32, (rows, cols, count), 0) + row_start
    ) * every_column + (lax.broadcasted_iota(jnp.int32, (rows, cols, count), 1) + col_start)
    cell = cell.reshape(rows * cols, count)
    next_row = (row_start + rows) * every_column + (
        lax.broadcasted_iota(jnp.int32, (cols, count), 0) + col_start
    )
    next_col = (lax.broadcasted_iota(jnp.int32, (rows, count), 0) + row_start) * every_column + (
        col_start + cols
    )
    for s in range(shots):
        record[s] = count_at(s, cell).reshape(rows, cols, depth)
        record_row[s] = count_at(s, next_row)
        record_col[s] = count_at(s, next_col)

    def motion(s):
        target, amplitude = source_cell[s], source_amp[s]

        def motion_row(x, carry):
            after = lax.rem(x + 1, rows)
            before = lax.rem(x + rows - 1, rows)
            last, first = x == rows - 1, x == 0
            buoyancy = 1.0 / density[x]
            scaled = COURANT * buoyancy
            change = density_change[x] * buoyancy
            accel = []
            for w in range(waves):
                sxx, syy, szz = st[s, w, 0, x], st[s, w, 1, x], st[s, w, 2, x]
                sxy, sxz, syz = st[s, w, 3, x], st[s, w, 4, x], st[s, w, 5, x]
                sxx_after = jnp.where(last, 0.0, st[s, w, 0, after])
                sxy_before = jnp.where(first, 0.0, st[s, w, 3, before])
                sxz_before = jnp.where(first, 0.0, st[s, w, 4, before])
                accel.append(
                    (
                        (sxx_after - sxx)
                        + (sxy - shifted_down(sxy, 0.0, 0))
                        + (sxz - shifted_down(sxz, 0.0, 1)),
                        (sxy - sxy_before)
                        + (shifted_up(syy, 0.0, 0) - syy)
                        + (syz - shifted_down(syz, 0.0, 1)),
                        (sxz - sxz_before)
                        + (syz - shifted_down(syz, 0.0, 0))
                        + (shifted_up(szz, 0.0, 1) - szz),
                    )
                )
            here = place + (x + row_start) * (every_column * depth)
            source = jnp.where(here == target, amplitude, 0.0)
            for c in range(3):
                first_wave = mo[s, 0, c, x] + scaled * accel[0][c]
                born = mo[s, 1, c, x] + scaled * (accel[1][c] - change * accel[0][c])
                adjoint = mo[s, 2, c, x] + scaled * accel[2][c]
                if c == 2:
                    first_wave = first_wave + scaled * source
                    adjoint = adjoint + scaled * record[s, x] * born
                accel0[s, c, x] = accel[0][c]
                mo[s, 0, c, x] = first_wave
                mo[s, 1, c, x] = born
                mo[s, 2, c, x] = adjoint
            return carry

        lax.fori_loop(0, rows, motion_row, 0, unroll=2)

    received(corners)
    for t, w in pairs:
        edge_out[0, line(slot(t, w, 0)), :] = corner_in[0, line(slot(t, w, 0)), :]
        edge_out[0, line(slot(t, w, 1)), :] = corner_in[0, line(slot(t, w, 1)), :]
        edge_out[0, line(slot(t, w, 2)), :] = corner_in[1, line(slot(t, w, 1)), :]
        edge_out[1, line(slot(t, w, 0)), :] = corner_in[1, line(slot(t, w, 0)), :]
        edge_out[1, line(slot(t, w, 1)), :] = corner_in[0, line(slot(t, w, 2)), :]
    send(edges)

    param_loads[0].wait()
    param_loads[1].wait()
    for s in range(shots):
        stress_loads[s].wait()
        motion_loads[s].wait()
        motion(s)
        if s == 0:
            received(first_hops)
            send(second_hops)

    low_face, up_face = (0, every), (rows - 1, every)
    left_face, right_face = (every, 0), (every, cols - 1)

    def fix_motion(s, where, c, message, at_spot, i, sign, parts=(True, True)):
        at = where + (every,)
        buoyancy = 1.0 / density[at]
        scaled = COURANT * buoyancy
        d0 = sign * message[at_spot(s, 0, i)]
        if parts[1]:
            change = density_change[at] * buoyancy
            born = scaled * (sign * message[at_spot(s, 1, i)] - change * d0)
            mo[(s, 1, c) + at] += born
        if parts[0]:
            accel0[(s, c) + at] += d0
            mo[(s, 0, c) + at] += scaled * d0
            adjoint = scaled * (sign * message[at_spot(s, 2, i)])
            if c == 2:
                adjoint = adjoint + scaled * record[(s,) + at] * born
            mo[(s, 2, c) + at] += adjoint

    side_index = lax.broadcasted_iota(jnp.int32, (rows, depth), 0)
    row_index = lax.broadcasted_iota(jnp.int32, (cols, depth), 0)

    def at_line(index, n, w, s, group, i):
        return jnp.where(index == n, edge_in[group, line(slot(s, w, i)), :], 0.0)

    def finish(s, message, at_spot, i, pushes, dst, field=None, which=(0, 1, 2)):
        scaled, change = scales(message)
        moved = {
            w: advance(scaled, change, w, message[at_spot(s, w, i)], pushes) for w in which
        }
        if field is not None:
            moved[2] = moved[2] + scaled * field * moved[1]
        for w in which:
            dst[w] = moved[w]

    def finish_left(s, cornered):
        pushes = [left_out[to_low(s, w, 0)] for w in range(waves)]
        if cornered:
            pushes = [d - at_line(side_index, 0, w, s, 1, 0) for w, d in enumerate(pushes)]
        finish(s, from_left, to_up, 2, pushes, left_halo.at[s])

    def finish_right(s, cornered):
        push_x = [-right_out[to_up(s, w, 0)] for w in range(waves)]
        push_z = [-right_out[to_up(s, w, 1)] for w in range(waves)]
        if cornered:
            push_x = [
                d + at_line(side_index, rows - 1, w, s, 0, 1) for w, d in enumerate(push_x)
            ]
            push_z = [d - at_line(side_index, 0, w, s, 0, 2) for w, d in enumerate(push_z)]
        finish(s, from_right, to_low, 1, push_x, right_halo.at[s, 0])
        finish(s, from_right, to_low, 2, push_z, right_halo.at[s, 1], record_col[s])

    def finish_low(s, which):
        pushes = [
            low_out[to_low(s, w, 0)] - at_line(row_index, 0, w, s, 1, 0) for w in range(waves)
        ]
        finish(s, from_low, to_up, 2, pushes, low_halo.at[s], None, which)

    def finish_up(s, which):
        push_y = [
            at_line(row_index, cols - 1, w, s, 0, 0) - up_out[to_up(s, w, 0)] for w in range(waves)
        ]
        finish(s, from_up, to_low, 1, push_y, up_halo.at[s, 0], None, which)
        if 0 in which:
            push_z = [
                -at_line(row_index, 0, w, s, 1, 1) - up_out[to_up(s, w, 1)] for w in range(waves)
            ]
            finish(s, from_up, to_low, 2, push_z, up_halo.at[s, 1], record_row[s])

    received(col_faces)

    @pl.when(has_up_y)
    def _():
        for s in range(shots):
            fix_motion(s, right_face, 1, from_right, to_low, 0, 1.0)
            finish_right(s, False)

    @pl.when(has_low_y)
    def _():
        for s in range(shots):
            fix_motion(s, left_face, 0, from_left, to_up, 0, -1.0)
            fix_motion(s, left_face, 2, from_left, to_up, 1, -1.0)
            finish_left(s, False)

    for copy in param_loads[2:]:
        copy.wait()

    def modulus(strain, first, second, twice):
        trace = first * (strain[0] + strain[1] + strain[2])
        return [trace + twice * strain[i] for i in range(3)] + [
            second * strain[i] for i in range(3, 6)
        ]

    def strain_of(s, w, x, lowest, highest):
        vx, vy, vz = mo[s, w, 0, x], mo[s, w, 1, x], mo[s, w, 2, x]
        vx_before = low_halo[s, w] if lowest else mo[s, w, 0, x - 1]
        vy_after = up_halo[s, 0, w] if highest else mo[s, w, 1, x + 1]
        vz_after = up_halo[s, 1, w] if highest else mo[s, w, 2, x + 1]
        vy_left = left_halo[s, w, line(x), :]
        vx_right = right_halo[s, 0, w, line(x), :]
        vz_right = right_halo[s, 1, w, line(x), :]
        return (
            vx - vx_before,
            vy - shifted_down(vy, vy_left, 0),
            vz - shifted_down(vz, 0.0, 1),
            (shifted_up(vx, vx_right, 0) - vx) + (vy_after - vy),
            (shifted_up(vx, 0.0, 1) - vx) + (vz_after - vz),
            (shifted_up(vy, 0.0, 1) - vy) + (shifted_up(vz, vz_right, 0) - vz),
        )

    def stress_row(s, x, lowest=False, highest=False, parts=(True, True)):
        first_modulus, second_modulus = lame[x], shear[x]
        twice = 2.0 * second_modulus
        e = strain_of(s, 0, x, lowest, highest)
        if parts[1]:
            second_change = shear_change[x]
            strain = strain_of(s, 1, x, lowest, highest)
            born = modulus(strain, first_modulus, second_modulus, twice)
            changed = modulus(e, lame_change[x], second_change, 2.0 * second_change)
            for c in range(6):
                st[s, 1, c, x] = st[s, 1, c, x] + COURANT * (born[c] + changed[c])
        if not parts[0]:
            return
        strain = strain_of(s, 2, x, lowest, highest)
        adjoint = modulus(strain, first_modulus, second_modulus, twice)
        a = []
        for c in range(6):
            a.append(st[s, 2, c, x] + COURANT * adjoint[c])
            st[s, 2, c, x] = a[c]
        total = (
            accel0[s, 0, x] * mo[s, 2, 0, x]
            + accel0[s, 1, x] * mo[s, 2, 1, x]
            + accel0[s, 2, x] * mo[s, 2, 2, x]
        )
        row_terms = (
            (e[0] + e[1] + e[2]) * (a[0] + a[1] + a[2]),
            2.0 * (e[0] * a[0] + e[1] * a[1] + e[2] * a[2])
            + e[3] * a[3]
            + e[4] * a[4]
            + e[5] * a[5],
            (1.0 / density[x]) * total,
        )
        for i in range(3):
            if lowest or highest:
                spare = edge_terms.at[0 if lowest else 1, i]
            else:
                spare = terms.at[i, x]
            spare[...] = row_terms[i] if s == 0 else spare[...] + row_terms[i]

    for s in range(shots):

        def inner_row(x, carry, s=s):
            stress_row(s, x)
            return carry

        lax.fori_loop(1, rows - 1, inner_row, 0, unroll=rows - 2)

    def share(src, dst, slot, peer):
        return pltpu.make_async_remote_copy(
            src_ref=src,
            dst_ref=dst,
            send_sem=share_send_sem.at[slot],
            recv_sem=share_recv_sem.at[slot],
            device_id={"shot": peer},
            device_id_type=MESH,
        )

    shares, edge_shares = [], []
    for k in range(1, groups):
        peer = lax.rem(me + k, groups)
        copy = share(terms.at[:, pl.ds(peer * own, own)], landed.at[k - 1], k - 1, peer)
        copy.start()
        shares.append(copy)
        for i, owner in enumerate((0, groups - 1)):
            copy = share(edge_terms.at[i], landed_edge.at[k - 1], groups + k - 2, owner)
            edge_shares.append((copy, peer == owner, me == owner))

    received(edges)

    @pl.when(has_up_y)
    def _():
        for s in range(shots):
            finish_right(s, True)

    @pl.when(has_low_y)
    def _():
        for s in range(shots):
            finish_left(s, True)

    received(row_faces)
    received(second_hops)

    @pl.when(has_up_x)
    def _():
        for s in range(shots):
            fix_motion(s, up_face, 0, from_up, to_low, 0, 1.0, (True, False))
            finish_up(s, (0, 2))

    @pl.when(has_low_x)
    def _():
        for s in range(shots):
            fix_motion(s, low_face, 1, from_low, to_up, 0, -1.0, (True, False))
            fix_motion(s, low_face, 2, from_low, to_up, 1, -1.0)
            finish_low(s, (0, 2))

    for s in range(shots):
        stress_row(s, 0, lowest=True, parts=(True, False))
        stress_row(s, rows - 1, highest=True, parts=(True, False))

    for copy, sends, _ in edge_shares:

        @pl.when(sends)
        def _(copy=copy):
            copy.start()

    received(born_faces)

    @pl.when(has_up_x)
    def _():
        for s in range(shots):
            fix_motion(s, up_face, 0, from_up, to_low, 0, 1.0, (False, True))
            finish_up(s, (1,))

    @pl.when(has_low_x)
    def _():
        for s in range(shots):
            fix_motion(s, low_face, 1, from_low, to_up, 0, -1.0, (False, True))
            finish_low(s, (1,))

    for s in range(shots):
        stress_row(s, 0, lowest=True, parts=(False, True))
        stress_row(s, rows - 1, highest=True, parts=(False, True))

    for copy in shares:
        copy.wait_recv()
    total = terms[:, pl.ds(me * own, own)]
    for k in range(1, groups):
        total = total + landed[k - 1]
    kernels[...] = total * (1.0 / total_shots)
    received(edge_shares)
    for i, owner, row in ((0, 0, 0), (1, groups - 1, own - 1)):

        @pl.when(me == owner)
        def _(i=i, row=row):
            total = edge_terms[i]
            for k in range(1, groups):
                total = total + landed_edge[k - 1]
            kernels[:, row] = total * (1.0 / total_shots)

    for copies in (row_faces, col_faces, born_faces, corners, edges, first_hops, second_hops, edge_shares):
        sent(copies)
    for copy in shares:
        copy.wait_send()


def write_kernel(st, mo, kernels_in, new_velocity, new_stress, kernels, sems):
    shots = st.shape[0]
    copies = [pltpu.make_async_copy(kernels_in, kernels, sems.at[2 * shots])]
    for s in range(shots):
        copies.append(
            pltpu.make_async_copy(st.at[s, pl.ds(1, 2)], new_stress.at[s], sems.at[2 * s])
        )
        copies.append(
            pltpu.make_async_copy(mo.at[s, pl.ds(1, 2)], new_velocity.at[s], sems.at[2 * s + 1])
        )
    for copy in copies:
        copy.start()
    for copy in copies:
        copy.wait()


def shards(
    stress_fields,
    velocity_fields,
    lame,
    shear,
    density,
    lame_change,
    shear_change,
    density_change,
    source_cell,
    source_amp,
    receiver_cell,
):
    rows, cols, depth = lame.shape
    shots, waves = stress_fields.shape[:2]
    groups = lax.axis_size("shot")
    own = rows // groups
    every_column = cols * lax.axis_size("gy")
    f32 = jnp.float32
    hbm = pl.BlockSpec(memory_space=pltpu.HBM)
    smem = pl.BlockSpec(memory_space=pltpu.SMEM)
    vmem = pl.BlockSpec(memory_space=pltpu.VMEM)
    row, col = (cols, depth), (rows, depth)
    message = shots * waves * 3 + 2
    lines = -(-shots * waves * 3 // 8) * 8
    scratch = [
        (6, rows, cols, depth),
        None,
        (shots, rows, cols, depth),
        (shots, *row),
        (shots, *col),
        (shots, 3, rows, cols, depth),
        (3, rows, cols, depth),
        (shots, waves, 6, *row),
        (shots, waves, 6, *row),
        (shots, waves, 6, *col),
        (shots, waves, 6, *col),
        (shots, waves, 2, *row),
        (shots, waves, *row),
        (2, shots, waves, *col),
        (shots, waves, *col),
        (message, *row),
        (message, *row),
        (message, *col),
        (message, *col),
        (message, *row),
        (message, *row),
        (message, *col),
        (message, *col),
        (RELAYED, *row),
        (2, lines, depth),
        (2, lines, depth),
        (2, lines, depth),
        (2, lines, depth),
        (shots, waves, *row),
        (shots, 2, waves, *row),
        (shots, waves, *col),
        (shots, 2, waves, *col),
        (2, 3, *row),
        (max(groups - 1, 1), 3, own, cols, depth),
        (max(groups - 1, 1), 3, *row),
    ]
    scratch = [
        pltpu.VMEM(receiver_cell.shape, jnp.int32) if dims is None else pltpu.VMEM(dims, f32)
        for dims in scratch
    ]
    st, mo, kernels = pl.pallas_call(
        functools.partial(step_kernel, every_column, shots * groups),
        name="step",
        out_shape=(
            pltpu.VMEM((shots, waves, 6, rows, cols, depth), f32),
            pltpu.VMEM((shots, waves, 3, rows, cols, depth), f32),
            pltpu.VMEM((3, own, cols, depth), f32),
        ),
        in_specs=[hbm] * 9 + [smem] * 2,
        out_specs=(vmem, vmem, vmem),
        scratch_shapes=scratch
        + [
            pltpu.SemaphoreType.DMA((shots, 2)),
            pltpu.SemaphoreType.DMA((17,)),
            pltpu.SemaphoreType.DMA((7,)),
            pltpu.SemaphoreType.DMA((16,)),
            pltpu.SemaphoreType.DMA((16,)),
            pltpu.SemaphoreType.DMA((max(2 * groups - 2, 1),)),
            pltpu.SemaphoreType.DMA((max(2 * groups - 2, 1),)),
        ],
        compiler_params=pltpu.CompilerParams(
            collective_id=0, has_side_effects=True, vmem_limit_bytes=VMEM_LIMIT
        ),
    )(
        *(
            pltpu.with_memory_space_constraint(array, pltpu.HBM)
            for array in (
                stress_fields,
                velocity_fields,
                lame,
                shear,
                density,
                lame_change,
                shear_change,
                density_change,
                receiver_cell,
                source_cell,
                source_amp,
            )
        ),
    )
    shape = lambda *dims: jax.ShapeDtypeStruct(dims, f32)
    return pl.pallas_call(
        write_kernel,
        name="write",
        out_shape=(
            shape(shots, 2, 3, rows, cols, depth),
            shape(shots, 2, 6, rows, cols, depth),
            shape(3, own, cols, depth),
        ),
        in_specs=[vmem] * 3,
        out_specs=(hbm, hbm, hbm),
        scratch_shapes=[pltpu.SemaphoreType.DMA((2 * shots + 1,))],
        compiler_params=pltpu.CompilerParams(vmem_limit_bytes=VMEM_LIMIT),
    )(st, mo, kernels)


def solution(mesh):
    return jax.shard_map(
        shards,
        mesh=mesh,
        in_specs=(
            P("shot", None, None, "gx", "gy", None),
            P("shot", None, None, "gx", "gy", None),
            P("gx", "gy", None),
            P("gx", "gy", None),
            P("gx", "gy", None),
            P("gx", "gy", None),
            P("gx", "gy", None),
            P("gx", "gy", None),
            P("shot"),
            P("shot"),
            P("shot", None),
        ),
        out_specs=(
            P("shot", None, None, "gx", "gy", None),
            P("shot", None, None, "gx", "gy", None),
            P(None, ("gx", "shot"), "gy", None),
        ),
        check_vma=False,
    )
```

```python
import functools

import jax
import jax.numpy as jnp
from jax import lax
from jax.experimental import pallas as pl
from jax.experimental.pallas import tpu as pltpu
from jax.sharding import PartitionSpec as P

RDEPTH = 2
COURANT = 0.25
MESH = pl.DeviceIdType.MESH
VMEM_LIMIT = 32 * 1024 * 1024
RELAYED = 12


def shifted_up(tile, halo, axis):
    length = tile.shape[axis]
    index = lax.broadcasted_iota(jnp.int32, tile.shape, axis)
    return jnp.where(index == length - 1, halo, pltpu.roll(tile, length - 1, axis))


def shifted_down(tile, halo, axis):
    index = lax.broadcasted_iota(jnp.int32, tile.shape, axis)
    return jnp.where(index == 0, halo, pltpu.roll(tile, 1, axis))


def step_kernel(
    every_column,
    total_shots,
    stress,
    velocity,
    lame_in,
    shear_in,
    density_in,
    lame_change_in,
    shear_change_in,
    density_change_in,
    receivers_in,
    source_cell,
    source_amp,
    st,
    mo,
    kernels,
    params,
    receivers,
    record,
    record_row,
    record_col,
    accel0,
    terms,
    first_stress,
    last_stress,
    left_stress,
    right_stress,
    first_motion,
    last_motion,
    left_motion,
    right_motion,
    low_out,
    up_out,
    left_out,
    right_out,
    from_up,
    from_low,
    from_right,
    from_left,
    relay,
    corner_out,
    corner_in,
    edge_out,
    edge_in,
    low_halo,
    up_halo,
    left_halo,
    right_halo,
    edge_terms,
    landed,
    landed_edge,
    load_sem,
    face_sem,
    param_sem,
    send_sem,
    recv_sem,
    share_send_sem,
    share_recv_sem,
):
    shots, waves, _, rows, cols, depth = stress.shape
    gx, gy = lax.axis_index("gx"), lax.axis_index("gy")
    nx, ny = lax.axis_size("gx"), lax.axis_size("gy")
    me, groups = lax.axis_index("shot"), lax.axis_size("shot")
    own = rows // groups
    has_low_x, has_up_x = gx > 0, gx < nx - 1
    has_low_y, has_up_y = gy > 0, gy < ny - 1
    sides = (
        (has_low_x, {"gx": gx - 1}),
        (has_up_x, {"gx": gx + 1}),
        (has_low_y, {"gy": gy - 1}),
        (has_up_y, {"gy": gy + 1}),
    )
    barrier = pltpu.get_barrier_semaphore()
    for present, device in sides:

        @pl.when(present)
        def _(device=device):
            pl.semaphore_signal(barrier, inc=1, device_id=device, device_id_type=MESH)

    if nx == 4 and groups == 2:
        for mid, source in ((0, 2), (3, 1)):

            @pl.when(gx == mid)
            def _(source=source):
                pl.semaphore_signal(barrier, inc=1, device_id={"gx": source}, device_id_type=MESH)

    for k in range(1, groups):
        peer = lax.rem(me + k, groups)
        pl.semaphore_signal(barrier, inc=1, device_id={"shot": peer}, device_id_type=MESH)

    tail = 2 + shots * 7
    faces = (
        (stress.at[:, :, :, 0], first_stress),
        (stress.at[:, :, :, rows - 1], last_stress),
        (velocity.at[:, :, pl.ds(1, 2), 0], first_motion),
        (velocity.at[:, :, 0, rows - 1], last_motion),
        (density_in.at[0], low_out.at[0]),
        (density_change_in.at[0], low_out.at[1]),
        (density_in.at[rows - 1], up_out.at[0]),
        (density_change_in.at[rows - 1], up_out.at[1]),
        (stress.at[:, :, :, :, 0], left_stress),
        (stress.at[:, :, :, :, cols - 1], right_stress),
        (velocity.at[:, :, 0, :, 0], left_motion.at[0]),
        (velocity.at[:, :, 2, :, 0], left_motion.at[1]),
        (velocity.at[:, :, 1, :, cols - 1], right_motion),
        (density_in.at[:, 0], left_out.at[0]),
        (density_change_in.at[:, 0], left_out.at[1]),
        (density_in.at[:, cols - 1], right_out.at[0]),
        (density_change_in.at[:, cols - 1], right_out.at[1]),
    )
    face_loads = [
        pltpu.make_async_copy(src, dst, face_sem.at[i]) for i, (src, dst) in enumerate(faces)
    ]
    stress_loads = [
        pltpu.make_async_copy(stress.at[s], st.at[s], load_sem.at[s, 0]) for s in range(shots)
    ]
    motion_loads = [
        pltpu.make_async_copy(velocity.at[s], mo.at[s], load_sem.at[s, 1]) for s in range(shots)
    ]
    receiver_load = pltpu.make_async_copy(receivers_in, receivers, param_sem.at[6])
    sources = (density_in, density_change_in, lame_in, shear_in, lame_change_in, shear_change_in)
    param_loads = [
        pltpu.make_async_copy(source, params.at[i], param_sem.at[i])
        for i, source in enumerate(sources)
    ]
    for copy in face_loads:
        copy.start()
    receiver_load.start()
    density, density_change, lame, shear, lame_change, shear_change = (
        params.at[i] for i in range(6)
    )

    def face(src, dst, slot, device):
        return pltpu.make_async_remote_copy(
            src_ref=src,
            dst_ref=dst,
            send_sem=send_sem.at[slot],
            recv_sem=recv_sem.at[slot],
            device_id=device,
            device_id_type=MESH,
        )

    low_x, up_x, low_y, up_y = (device for _, device in sides)
    body, rest = pl.ds(0, tail), pl.ds(tail, shots * 2)
    direct = pl.ds(0, tail + shots * 2 - RELAYED)
    detour = pl.ds(tail + shots * 2 - RELAYED, RELAYED)
    relays = nx == 4 and groups == 2
    at_column = [jnp.logical_and(relays, gx == i) for i in range(4)]
    plain_low, plain_up = (
        jnp.logical_and(has_low_x, jnp.logical_not(at_column[2])),
        jnp.logical_and(has_up_x, jnp.logical_not(at_column[1])),
    )
    row_faces = (
        (face(low_out.at[body], from_up.at[body], 0, low_x), plain_low, plain_up),
        (face(up_out.at[body], from_low.at[body], 1, up_x), plain_up, plain_low),
    )
    born_faces = (
        (face(low_out.at[rest], from_up.at[rest], 8, low_x), plain_low, plain_up),
        (face(up_out.at[rest], from_low.at[rest], 9, up_x), plain_up, plain_low),
    )
    first_hops, second_hops = (), ()
    if relays:
        row_faces += (
            (face(low_out.at[direct], from_up.at[direct], 10, low_x), at_column[2], at_column[1]),
            (face(up_out.at[direct], from_low.at[direct], 11, up_x), at_column[1], at_column[2]),
        )
        first_hops = (
            (face(low_out.at[detour], relay, 12, {"gx": 0}), at_column[2], at_column[0]),
            (face(up_out.at[detour], relay, 13, {"gx": 3}), at_column[1], at_column[3]),
        )
        second_hops = (
            (face(relay, from_up.at[detour], 14, {"gx": 1}), at_column[0], at_column[1]),
            (face(relay, from_low.at[detour], 15, {"gx": 2}), at_column[3], at_column[2]),
        )
    col_faces = []
    for s in range(shots):
        first_tile = 2 + s * waves * 3 if s else 0
        part = pl.ds(first_tile, 2 + (s + 1) * waves * 3 - first_tile)
        col_faces.append(
            (
                (
                    face(left_out.at[part], from_right.at[part], 16 + 2 * s, low_y),
                    has_low_y,
                    has_up_y,
                ),
                (
                    face(right_out.at[part], from_left.at[part], 17 + 2 * s, up_y),
                    has_up_y,
                    has_low_y,
                ),
            )
        )
    corners = (
        (face(corner_out.at[0], corner_in.at[0], 4, low_x), has_low_x, has_up_x),
        (face(corner_out.at[1], corner_in.at[1], 5, up_x), has_up_x, has_low_x),
    )
    edges = (
        (face(edge_out.at[0], edge_in.at[0], 6, low_y), has_low_y, has_up_y),
        (face(edge_out.at[1], edge_in.at[1], 7, up_y), has_up_y, has_low_y),
    )

    def send(faces):
        for copy, sends, _ in faces:

            @pl.when(sends)
            def _(copy=copy):
                copy.start()

    def sent(faces):
        for copy, sends, _ in faces:

            @pl.when(sends)
            def _(copy=copy):
                copy.wait_send()

    def received(faces):
        for copy, _, comes in faces:

            @pl.when(comes)
            def _(copy=copy):
                copy.wait_recv()

    row_start, col_start = gx * rows, gy * cols
    pairs = [(s, w) for s in range(shots) for w in range(waves)]
    every = slice(None)

    def slot(s, w, i):
        return (s * waves + w) * 3 + i

    def spot(s, w, i, early):
        if w != 1:
            return 2 + ((w // 2) * shots + s) * 3 + i
        if i == early:
            return 2 + shots * 6 + s
        return tail + s * 2 + i // (3 - early)

    def by_shot(s, w, i):
        return 2 + slot(s, w, i)

    def to_low(s, w, i):
        return spot(s, w, i, 2)

    def to_up(s, w, i):
        return spot(s, w, i, 1)

    def scales(message):
        buoyancy = 1.0 / message[0]
        return COURANT * buoyancy, message[1] * buoyancy

    def source_of(s, here):
        return jnp.where(here == source_cell[s], source_amp[s], 0.0)

    def advance(scaled, change, w, start, push):
        if w == 1:
            return start + scaled * (push[1] - change * push[0])
        return start + scaled * push[w]

    place = (
        lax.broadcasted_iota(jnp.int32, (cols, depth), 0) + col_start
    ) * depth + lax.broadcasted_iota(jnp.int32, (cols, depth), 1)
    side_place = (
        (lax.broadcasted_iota(jnp.int32, (rows, depth), 0) + row_start) * every_column + col_start
    ) * depth + lax.broadcasted_iota(jnp.int32, (rows, depth), 1)

    for copy in face_loads[:8]:
        copy.wait()
    low_scales, up_scales = scales(low_out), scales(up_out)
    for s in range(shots):
        push_y, push_z, push_x = [], [], []
        for w in range(waves):
            sxx, syy, szz, sxy, sxz, syz = (first_stress[s, w, i] for i in range(6))
            low_out[to_low(s, w, 0)] = sxx
            push_y.append(sxy + (shifted_up(syy, 0.0, 0) - syy) + (syz - shifted_down(syz, 0.0, 1)))
            push_z.append(sxz + (syz - shifted_down(syz, 0.0, 0)) + (shifted_up(szz, 0.0, 1) - szz))
            sxx, sxy, sxz = (last_stress[s, w, i] for i in (0, 3, 4))
            up_out[to_up(s, w, 0)] = sxy
            up_out[to_up(s, w, 1)] = sxz
            push_x.append((sxy - shifted_down(sxy, 0.0, 0)) + (sxz - shifted_down(sxz, 0.0, 1)) - sxx)
        here = place + row_start * (every_column * depth)
        for w in range(waves):
            low_out[to_low(s, w, 1)] = advance(*low_scales, w, first_motion[s, w, 0], push_y)
            moved = advance(*low_scales, w, first_motion[s, w, 1], push_z)
            if w == 0:
                moved = moved + low_scales[0] * source_of(s, here)
            low_out[to_low(s, w, 2)] = moved
            up_out[to_up(s, w, 2)] = advance(*up_scales, w, last_motion[s, w], push_x)

    for copy in face_loads[8:]:
        copy.wait()
    left_scales, right_scales = scales(left_out), scales(right_out)
    for s in range(shots):
        push_x, push_z, push_y = [], [], []
        for w in range(waves):
            sxx, syy, szz, sxy, sxz, syz = (left_stress[s, w, i] for i in range(6))
            left_out[by_shot(s, w, 0)] = syy
            push_x.append((shifted_up(sxx, 0.0, 0) - sxx) + sxy + (sxz - shifted_down(sxz, 0.0, 1)))
            push_z.append((sxz - shifted_down(sxz, 0.0, 0)) + syz + (shifted_up(szz, 0.0, 1) - szz))
            syy, sxy, syz = (right_stress[s, w, i] for i in (1, 3, 5))
            right_out[by_shot(s, w, 0)] = sxy
            right_out[by_shot(s, w, 1)] = syz
            push_y.append((sxy - shifted_down(sxy, 0.0, 0)) + (syz - shifted_down(syz, 0.0, 1)) - syy)
        for w in range(waves):
            left_out[by_shot(s, w, 1)] = advance(*left_scales, w, left_motion[0, s, w], push_x)
            moved = advance(*left_scales, w, left_motion[1, s, w], push_z)
            if w == 0:
                moved = moved + left_scales[0] * source_of(s, side_place)
            left_out[by_shot(s, w, 2)] = moved
            right_out[by_shot(s, w, 2)] = advance(*right_scales, w, right_motion[s, w], push_y)

    def line(n):
        return pl.ds(n, 1)

    first, last = line(0), line(cols - 1)
    for s, w in pairs:
        corner_out[0, line(slot(s, w, 0)), :] = first_stress[s, w, 1, first, :]
        corner_out[0, line(slot(s, w, 1)), :] = first_stress[s, w, 0, first, :]
        corner_out[0, line(slot(s, w, 2)), :] = first_stress[s, w, 5, last, :]
        corner_out[1, line(slot(s, w, 0)), :] = last_stress[s, w, 3, last, :]
        corner_out[1, line(slot(s, w, 1)), :] = last_stress[s, w, 4, first, :]

    neighbours = groups - 1
    for present, _ in sides:
        neighbours = neighbours + present.astype(jnp.int32)
    if relays:
        neighbours = neighbours + jnp.logical_or(gx == 1, gx == 2).astype(jnp.int32)
    pl.semaphore_wait(barrier, neighbours)
    send(corners)
    send(first_hops)
    send(row_faces)
    for s in range(shots):
        send(col_faces[s])
    send(born_faces)
    param_loads[0].start()
    param_loads[1].start()
    for s in range(shots):
        stress_loads[s].start()
        motion_loads[s].start()
    for copy in param_loads[2:]:
        copy.start()

    for comes, ref in (
        (has_up_x, corner_in.at[0]),
        (has_low_x, corner_in.at[1]),
        (has_up_y, edge_in.at[0]),
        (has_low_y, edge_in.at[1]),
        (has_up_x, up_halo),
        (has_low_x, low_halo),
        (has_up_y, right_halo),
        (has_low_y, left_halo),
    ):

        @pl.when(jnp.logical_not(comes))
        def _(ref=ref):
            ref[...] = jnp.zeros(ref.shape, jnp.float32)

    for x in (0, rows - 1):
        terms[:, x] = jnp.zeros((3, cols, depth), jnp.float32)

    receiver_load.wait()
    count = receivers.shape[1]
    plane = (lax.broadcasted_iota(jnp.int32, (count, depth), 1) == RDEPTH).astype(jnp.bfloat16)

    def count_at(s, cell):
        marks = jnp.where(receivers[pl.ds(s, 1), :] == cell, 1.0, 0.0).astype(jnp.bfloat16)
        return jnp.dot(marks, plane, preferred_element_type=jnp.float32)

    cell = (
        lax.broadcasted_iota(jnp.int32, (rows, cols, count), 0) + row_start
    ) * every_column + (lax.broadcasted_iota(jnp.int32, (rows, cols, count), 1) + col_start)
    cell = cell.reshape(rows * cols, count)
    next_row = (row_start + rows) * every_column + (
        lax.broadcasted_iota(jnp.int32, (cols, count), 0) + col_start
    )
    next_col = (lax.broadcasted_iota(jnp.int32, (rows, count), 0) + row_start) * every_column + (
        col_start + cols
    )
    for s in range(shots):
        record[s] = count_at(s, cell).reshape(rows, cols, depth)
        record_row[s] = count_at(s, next_row)
        record_col[s] = count_at(s, next_col)

    def motion(s):
        target, amplitude = source_cell[s], source_amp[s]

        def motion_row(x, carry):
            after = lax.rem(x + 1, rows)
            before = lax.rem(x + rows - 1, rows)
            last, first = x == rows - 1, x == 0
            buoyancy = 1.0 / density[x]
            scaled = COURANT * buoyancy
            change = density_change[x] * buoyancy
            accel = []
            for w in range(waves):
                sxx, syy, szz = st[s, w, 0, x], st[s, w, 1, x], st[s, w, 2, x]
                sxy, sxz, syz = st[s, w, 3, x], st[s, w, 4, x], st[s, w, 5, x]
                sxx_after = jnp.where(last, 0.0, st[s, w, 0, after])
                sxy_before = jnp.where(first, 0.0, st[s, w, 3, before])
                sxz_before = jnp.where(first, 0.0, st[s, w, 4, before])
                accel.append(
                    (
                        (sxx_after - sxx)
                        + (sxy - shifted_down(sxy, 0.0, 0))
                        + (sxz - shifted_down(sxz, 0.0, 1)),
                        (sxy - sxy_before)
                        + (shifted_up(syy, 0.0, 0) - syy)
                        + (syz - shifted_down(syz, 0.0, 1)),
                        (sxz - sxz_before)
                        + (syz - shifted_down(syz, 0.0, 0))
                        + (shifted_up(szz, 0.0, 1) - szz),
                    )
                )
            here = place + (x + row_start) * (every_column * depth)
            source = jnp.where(here == target, amplitude, 0.0)
            for c in range(3):
                first_wave = mo[s, 0, c, x] + scaled * accel[0][c]
                born = mo[s, 1, c, x] + scaled * (accel[1][c] - change * accel[0][c])
                adjoint = mo[s, 2, c, x] + scaled * accel[2][c]
                if c == 2:
                    first_wave = first_wave + scaled * source
                    adjoint = adjoint + scaled * record[s, x] * born
                accel0[s, c, x] = accel[0][c]
                mo[s, 0, c, x] = first_wave
                mo[s, 1, c, x] = born
                mo[s, 2, c, x] = adjoint
            return carry

        lax.fori_loop(0, rows, motion_row, 0, unroll=2)

    received(corners)
    for t, w in pairs:
        edge_out[0, line(slot(t, w, 0)), :] = corner_in[0, line(slot(t, w, 0)), :]
        edge_out[0, line(slot(t, w, 1)), :] = corner_in[0, line(slot(t, w, 1)), :]
        edge_out[0, line(slot(t, w, 2)), :] = corner_in[1, line(slot(t, w, 1)), :]
        edge_out[1, line(slot(t, w, 0)), :] = corner_in[1, line(slot(t, w, 0)), :]
        edge_out[1, line(slot(t, w, 1)), :] = corner_in[0, line(slot(t, w, 2)), :]
    send(edges)

    param_loads[0].wait()
    param_loads[1].wait()
    for s in range(shots):
        stress_loads[s].wait()
        motion_loads[s].wait()
        motion(s)
        if s == 0:
            received(first_hops)
            send(second_hops)

    low_face, up_face = (0, every), (rows - 1, every)
    left_face, right_face = (every, 0), (every, cols - 1)

    def fix_motion(s, where, c, message, at_spot, i, sign, parts=(True, True)):
        at = where + (every,)
        buoyancy = 1.0 / density[at]
        scaled = COURANT * buoyancy
        d0 = sign * message[at_spot(s, 0, i)]
        if parts[1]:
            change = density_change[at] * buoyancy
            born = scaled * (sign * message[at_spot(s, 1, i)] - change * d0)
            mo[(s, 1, c) + at] += born
        if parts[0]:
            accel0[(s, c) + at] += d0
            mo[(s, 0, c) + at] += scaled * d0
            adjoint = scaled * (sign * message[at_spot(s, 2, i)])
            if c == 2:
                adjoint = adjoint + scaled * record[(s,) + at] * born
            mo[(s, 2, c) + at] += adjoint

    side_index = lax.broadcasted_iota(jnp.int32, (rows, depth), 0)
    row_index = lax.broadcasted_iota(jnp.int32, (cols, depth), 0)

    def at_line(index, n, w, s, group, i):
        return jnp.where(index == n, edge_in[group, line(slot(s, w, i)), :], 0.0)

    def finish(s, message, at_spot, i, pushes, dst, field=None, which=(0, 1, 2)):
        scaled, change = scales(message)
        moved = {
            w: advance(scaled, change, w, message[at_spot(s, w, i)], pushes) for w in which
        }
        if field is not None:
            moved[2] = moved[2] + scaled * field * moved[1]
        for w in which:
            dst[w] = moved[w]

    def finish_left(s, cornered):
        pushes = [left_out[by_shot(s, w, 0)] for w in range(waves)]
        if cornered:
            pushes = [d - at_line(side_index, 0, w, s, 1, 0) for w, d in enumerate(pushes)]
        finish(s, from_left, by_shot, 2, pushes, left_halo.at[s])

    def finish_right(s, cornered):
        push_x = [-right_out[by_shot(s, w, 0)] for w in range(waves)]
        push_z = [-right_out[by_shot(s, w, 1)] for w in range(waves)]
        if cornered:
            push_x = [
                d + at_line(side_index, rows - 1, w, s, 0, 1) for w, d in enumerate(push_x)
            ]
            push_z = [d - at_line(side_index, 0, w, s, 0, 2) for w, d in enumerate(push_z)]
        finish(s, from_right, by_shot, 1, push_x, right_halo.at[s, 0])
        finish(s, from_right, by_shot, 2, push_z, right_halo.at[s, 1], record_col[s])

    def finish_low(s, which):
        pushes = [
            low_out[to_low(s, w, 0)] - at_line(row_index, 0, w, s, 1, 0) for w in range(waves)
        ]
        finish(s, from_low, to_up, 2, pushes, low_halo.at[s], None, which)

    def finish_up(s, which):
        push_y = [
            at_line(row_index, cols - 1, w, s, 0, 0) - up_out[to_up(s, w, 0)] for w in range(waves)
        ]
        finish(s, from_up, to_low, 1, push_y, up_halo.at[s, 0], None, which)
        if 0 in which:
            push_z = [
                -at_line(row_index, 0, w, s, 1, 1) - up_out[to_up(s, w, 1)] for w in range(waves)
            ]
            finish(s, from_up, to_low, 2, push_z, up_halo.at[s, 1], record_row[s])

    for copy in param_loads[2:]:
        copy.wait()

    def modulus(strain, first, second, twice):
        trace = first * (strain[0] + strain[1] + strain[2])
        return [trace + twice * strain[i] for i in range(3)] + [
            second * strain[i] for i in range(3, 6)
        ]

    def strain_of(s, w, x, lowest, highest):
        vx, vy, vz = mo[s, w, 0, x], mo[s, w, 1, x], mo[s, w, 2, x]
        vx_before = low_halo[s, w] if lowest else mo[s, w, 0, x - 1]
        vy_after = up_halo[s, 0, w] if highest else mo[s, w, 1, x + 1]
        vz_after = up_halo[s, 1, w] if highest else mo[s, w, 2, x + 1]
        vy_left = left_halo[s, w, line(x), :]
        vx_right = right_halo[s, 0, w, line(x), :]
        vz_right = right_halo[s, 1, w, line(x), :]
        return (
            vx - vx_before,
            vy - shifted_down(vy, vy_left, 0),
            vz - shifted_down(vz, 0.0, 1),
            (shifted_up(vx, vx_right, 0) - vx) + (vy_after - vy),
            (shifted_up(vx, 0.0, 1) - vx) + (vz_after - vz),
            (shifted_up(vy, 0.0, 1) - vy) + (shifted_up(vz, vz_right, 0) - vz),
        )

    def stress_row(s, x, lowest=False, highest=False, parts=(True, True)):
        first_modulus, second_modulus = lame[x], shear[x]
        twice = 2.0 * second_modulus
        e = strain_of(s, 0, x, lowest, highest)
        if parts[1]:
            second_change = shear_change[x]
            strain = strain_of(s, 1, x, lowest, highest)
            born = modulus(strain, first_modulus, second_modulus, twice)
            changed = modulus(e, lame_change[x], second_change, 2.0 * second_change)
            for c in range(6):
                st[s, 1, c, x] = st[s, 1, c, x] + COURANT * (born[c] + changed[c])
        if not parts[0]:
            return
        strain = strain_of(s, 2, x, lowest, highest)
        adjoint = modulus(strain, first_modulus, second_modulus, twice)
        a = []
        for c in range(6):
            a.append(st[s, 2, c, x] + COURANT * adjoint[c])
            st[s, 2, c, x] = a[c]
        total = (
            accel0[s, 0, x] * mo[s, 2, 0, x]
            + accel0[s, 1, x] * mo[s, 2, 1, x]
            + accel0[s, 2, x] * mo[s, 2, 2, x]
        )
        row_terms = (
            (e[0] + e[1] + e[2]) * (a[0] + a[1] + a[2]),
            2.0 * (e[0] * a[0] + e[1] * a[1] + e[2] * a[2])
            + e[3] * a[3]
            + e[4] * a[4]
            + e[5] * a[5],
            (1.0 / density[x]) * total,
        )
        for i in range(3):
            if lowest or highest:
                spare = edge_terms.at[0 if lowest else 1, i]
            else:
                spare = terms.at[i, x]
            spare[...] = row_terms[i] if s == 0 else spare[...] + row_terms[i]

    for s in range(shots):
        received(col_faces[s])

        @pl.when(has_up_y)
        def _(s=s):
            fix_motion(s, right_face, 1, from_right, by_shot, 0, 1.0)
            finish_right(s, False)

        @pl.when(has_low_y)
        def _(s=s):
            fix_motion(s, left_face, 0, from_left, by_shot, 0, -1.0)
            fix_motion(s, left_face, 2, from_left, by_shot, 1, -1.0)
            finish_left(s, False)

        def inner_row(x, carry, s=s):
            stress_row(s, x)
            return carry

        lax.fori_loop(1, rows - 1, inner_row, 0, unroll=rows - 2)

    def share(src, dst, slot, peer):
        return pltpu.make_async_remote_copy(
            src_ref=src,
            dst_ref=dst,
            send_sem=share_send_sem.at[slot],
            recv_sem=share_recv_sem.at[slot],
            device_id={"shot": peer},
            device_id_type=MESH,
        )

    shares, edge_shares = [], []
    for k in range(1, groups):
        peer = lax.rem(me + k, groups)
        copy = share(terms.at[:, pl.ds(peer * own, own)], landed.at[k - 1], k - 1, peer)
        copy.start()
        shares.append(copy)
        for i, owner in enumerate((0, groups - 1)):
            copy = share(edge_terms.at[i], landed_edge.at[k - 1], groups + k - 2, owner)
            edge_shares.append((copy, peer == owner, me == owner))

    received(edges)

    @pl.when(has_up_y)
    def _():
        for s in range(shots):
            finish_right(s, True)

    @pl.when(has_low_y)
    def _():
        for s in range(shots):
            finish_left(s, True)

    received(row_faces)
    received(second_hops)

    @pl.when(has_up_x)
    def _():
        for s in range(shots):
            fix_motion(s, up_face, 0, from_up, to_low, 0, 1.0, (True, False))
            finish_up(s, (0, 2))

    @pl.when(has_low_x)
    def _():
        for s in range(shots):
            fix_motion(s, low_face, 1, from_low, to_up, 0, -1.0, (True, False))
            fix_motion(s, low_face, 2, from_low, to_up, 1, -1.0)
            finish_low(s, (0, 2))

    for s in range(shots):
        stress_row(s, 0, lowest=True, parts=(True, False))
        stress_row(s, rows - 1, highest=True, parts=(True, False))

    for copy, sends, _ in edge_shares:

        @pl.when(sends)
        def _(copy=copy):
            copy.start()

    received(born_faces)

    @pl.when(has_up_x)
    def _():
        for s in range(shots):
            fix_motion(s, up_face, 0, from_up, to_low, 0, 1.0, (False, True))
            finish_up(s, (1,))

    @pl.when(has_low_x)
    def _():
        for s in range(shots):
            fix_motion(s, low_face, 1, from_low, to_up, 0, -1.0, (False, True))
            finish_low(s, (1,))

    for s in range(shots):
        stress_row(s, 0, lowest=True, parts=(False, True))
        stress_row(s, rows - 1, highest=True, parts=(False, True))

    for copy in shares:
        copy.wait_recv()
    total = terms[:, pl.ds(me * own, own)]
    for k in range(1, groups):
        total = total + landed[k - 1]
    kernels[...] = total * (1.0 / total_shots)
    received(edge_shares)
    for i, owner, row in ((0, 0, 0), (1, groups - 1, own - 1)):

        @pl.when(me == owner)
        def _(i=i, row=row):
            total = edge_terms[i]
            for k in range(1, groups):
                total = total + landed_edge[k - 1]
            kernels[:, row] = total * (1.0 / total_shots)

    for copies in (row_faces, *col_faces, born_faces, corners, edges, first_hops, second_hops, edge_shares):
        sent(copies)
    for copy in shares:
        copy.wait_send()


def write_kernel(st, mo, kernels_in, new_velocity, new_stress, kernels, sems):
    shots = st.shape[0]
    copies = [pltpu.make_async_copy(kernels_in, kernels, sems.at[2 * shots])]
    for s in range(shots):
        copies.append(
            pltpu.make_async_copy(st.at[s, pl.ds(1, 2)], new_stress.at[s], sems.at[2 * s])
        )
        copies.append(
            pltpu.make_async_copy(mo.at[s, pl.ds(1, 2)], new_velocity.at[s], sems.at[2 * s + 1])
        )
    for copy in copies:
        copy.start()
    for copy in copies:
        copy.wait()


def shards(
    stress_fields,
    velocity_fields,
    lame,
    shear,
    density,
    lame_change,
    shear_change,
    density_change,
    source_cell,
    source_amp,
    receiver_cell,
):
    rows, cols, depth = lame.shape
    shots, waves = stress_fields.shape[:2]
    groups = lax.axis_size("shot")
    own = rows // groups
    every_column = cols * lax.axis_size("gy")
    f32 = jnp.float32
    hbm = pl.BlockSpec(memory_space=pltpu.HBM)
    smem = pl.BlockSpec(memory_space=pltpu.SMEM)
    vmem = pl.BlockSpec(memory_space=pltpu.VMEM)
    row, col = (cols, depth), (rows, depth)
    message = shots * waves * 3 + 2
    lines = -(-shots * waves * 3 // 8) * 8
    scratch = [
        (6, rows, cols, depth),
        None,
        (shots, rows, cols, depth),
        (shots, *row),
        (shots, *col),
        (shots, 3, rows, cols, depth),
        (3, rows, cols, depth),
        (shots, waves, 6, *row),
        (shots, waves, 6, *row),
        (shots, waves, 6, *col),
        (shots, waves, 6, *col),
        (shots, waves, 2, *row),
        (shots, waves, *row),
        (2, shots, waves, *col),
        (shots, waves, *col),
        (message, *row),
        (message, *row),
        (message, *col),
        (message, *col),
        (message, *row),
        (message, *row),
        (message, *col),
        (message, *col),
        (RELAYED, *row),
        (2, lines, depth),
        (2, lines, depth),
        (2, lines, depth),
        (2, lines, depth),
        (shots, waves, *row),
        (shots, 2, waves, *row),
        (shots, waves, *col),
        (shots, 2, waves, *col),
        (2, 3, *row),
        (max(groups - 1, 1), 3, own, cols, depth),
        (max(groups - 1, 1), 3, *row),
    ]
    scratch = [
        pltpu.VMEM(receiver_cell.shape, jnp.int32) if dims is None else pltpu.VMEM(dims, f32)
        for dims in scratch
    ]
    st, mo, kernels = pl.pallas_call(
        functools.partial(step_kernel, every_column, shots * groups),
        name="step",
        out_shape=(
            pltpu.VMEM((shots, waves, 6, rows, cols, depth), f32),
            pltpu.VMEM((shots, waves, 3, rows, cols, depth), f32),
            pltpu.VMEM((3, own, cols, depth), f32),
        ),
        in_specs=[hbm] * 9 + [smem] * 2,
        out_specs=(vmem, vmem, vmem),
        scratch_shapes=scratch
        + [
            pltpu.SemaphoreType.DMA((shots, 2)),
            pltpu.SemaphoreType.DMA((17,)),
            pltpu.SemaphoreType.DMA((7,)),
            pltpu.SemaphoreType.DMA((16 + 2 * shots,)),
            pltpu.SemaphoreType.DMA((16 + 2 * shots,)),
            pltpu.SemaphoreType.DMA((max(2 * groups - 2, 1),)),
            pltpu.SemaphoreType.DMA((max(2 * groups - 2, 1),)),
        ],
        compiler_params=pltpu.CompilerParams(
            collective_id=0, has_side_effects=True, vmem_limit_bytes=VMEM_LIMIT
        ),
    )(
        *(
            pltpu.with_memory_space_constraint(array, pltpu.HBM)
            for array in (
                stress_fields,
                velocity_fields,
                lame,
                shear,
                density,
                lame_change,
                shear_change,
                density_change,
                receiver_cell,
                source_cell,
                source_amp,
            )
        ),
    )
    shape = lambda *dims: jax.ShapeDtypeStruct(dims, f32)
    return pl.pallas_call(
        write_kernel,
        name="write",
        out_shape=(
            shape(shots, 2, 3, rows, cols, depth),
            shape(shots, 2, 6, rows, cols, depth),
            shape(3, own, cols, depth),
        ),
        in_specs=[vmem] * 3,
        out_specs=(hbm, hbm, hbm),
        scratch_shapes=[pltpu.SemaphoreType.DMA((2 * shots + 1,))],
        compiler_params=pltpu.CompilerParams(vmem_limit_bytes=VMEM_LIMIT),
    )(st, mo, kernels)


def solution(mesh):
    return jax.shard_map(
        shards,
        mesh=mesh,
        in_specs=(
            P("shot", None, None, "gx", "gy", None),
            P("shot", None, None, "gx", "gy", None),
            P("gx", "gy", None),
            P("gx", "gy", None),
            P("gx", "gy", None),
            P("gx", "gy", None),
            P("gx", "gy", None),
            P("gx", "gy", None),
            P("shot"),
            P("shot"),
            P("shot", None),
        ),
        out_specs=(
            P("shot", None, None, "gx", "gy", None),
            P("shot", None, None, "gx", "gy", None),
            P(None, ("gx", "shot"), "gy", None),
        ),
        check_vma=False,
    )
```
